32 devices in a mesh: expert: 8 (over z, y), tensor: 4 (over x, core).
Axes of the slice: x: 2, y: 2, z: 4, core: 2. Of those that a mesh axis runs over, the one named last changes fastest.
Arguments:
- tokens: bfloat16 [3152, 768], P('expert'), may hold values from -6 to 6
- norm1_gain: float32 [768], replicated, may hold values from 0.5 to 1.5
- norm1_shift: float32 [768], replicated, may hold values from -4 to 4
- qkv_weight: bfloat16 [768, 2304], P(None, 'tensor'), may hold values from -3 to 3
- proj_weight: bfloat16 [768, 768], P('tensor'), may hold values from -1.75 to 1.75
- proj_shift: float32 [768], replicated, may hold values from -6 to 6
- norm2_gain: float32 [768], replicated, may hold values from 0.5 to 1.5
- norm2_shift: float32 [768], replicated, may hold values from -4 to 4
- router_weight: bfloat16 [768, 8], replicated, may hold values from -8 to 8
- expand_weight: bfloat16 [8, 768, 3072], P('expert', None, 'tensor'), may hold values from -0.21875 to 0.21875
- expand_shift: float32 [8, 3072], P('expert', 'tensor'), may hold values from -6 to 6
- shrink_weight: bfloat16 [8, 3072, 768], P('expert', 'tensor'), may hold values from -0.109375 to 0.109375
- shrink_shift: float32 [8, 768], P('expert'), may hold values from -4 to 4
- route_expert: int32 [3152, 2], P('expert'), may hold values from 0 to 7, as said below
- route_slot: int32 [3152, 2], P('expert'), may hold values from -1 to 123, as said below
- cotangent: bfloat16 [3152, 768], P('expert'), may hold values from -6 to 6
Outputs:
- output: float32 [3152, 768], P('expert')
- tokens_grad: float32 [3152, 768], P('expert')
- gain1_grad: float32 [768], replicated
- shift1_grad: float32 [768], replicated
- qkv_grad: float32 [768, 2304], P(None, 'tensor')
- proj_grad: float32 [768, 768], P('tensor')
- pshift_grad: float32 [768], replicated
- gain2_grad: float32 [768], replicated
- shift2_grad: float32 [768], replicated
- router_grad: float32 [768, 8], replicated
- expand_grad: float32 [8, 768, 3072], P('expert', None, 'tensor')
- eshift_grad: float32 [8, 3072], P('expert', 'tensor')
- shrink_grad: float32 [8, 3072, 768], P('expert', 'tensor')
- sshift_grad: float32 [8, 768], P('expert')
The draws below stay inside these ranges and needn't reach their ends.
Inputs may be any that keep to these rules, and one draw needn't show every extreme that they name: `route_expert`: each row names two different experts. In some expert's column more than 124 first choices fall in the rows of one device, in every draw. `route_slot`: within the rows of one device and for each expert, the first choices of all rows in row order and then the second choices in row order take slots 0, 1, 2, ... of that expert; once 124 slots are taken, further choices of it get -1. Some expert has all 124 slots taken in every device's rows, in every draw.
All inputs are finite; a program needn't handle non-finite values.
Results may differ from the reference program's by a relative error of at most 0.03.
Values may be sent and summed in bfloat16 or wider, within the bound.
A program may use at most 128 MiB of HBM per device.

```python
import jax
import jax.numpy as jnp
from jax import lax

D = 768
H = 12
DH = 64
FF = 3072
SEQ = 197
IMG_DEV = 2
TOK_DEV = 394
TOKENS = 3152
EXPERTS = 8
CAP = 124
N_TENSOR = 4


def route_pair(key):
    blocks = TOKENS // TOK_DEV
    first_key = jax.random.fold_in(key, 101)
    second_key = jax.random.fold_in(key, 202)
    label_key = jax.random.fold_in(key, 303)
    order_key = jax.random.fold_in(key, 404)
    other_key = jax.random.fold_in(key, 505)
    raw_pick = jax.random.randint(first_key, (TOKENS,), 0, EXPERTS) * jax.random.randint(second_key, (TOKENS,), 0, EXPERTS) // EXPERTS
    relabel = jax.random.permutation(label_key, EXPERTS).astype(jnp.int32)
    first_choice = relabel[raw_pick]

    def block_order(block_key):
        return jax.random.permutation(block_key, TOK_DEV)
    orders = jax.vmap(block_order)(jax.random.split(order_key, blocks))
    ranks = jnp.argsort(orders, axis=1)
    forced = (ranks < CAP + 2).reshape(TOKENS)
    first_choice = jnp.where(forced, relabel[0], first_choice)
    second_choice = (first_choice + 1 + jax.random.randint(other_key, (TOKENS,), 0, EXPERTS - 1)) % EXPERTS
    expert_ids = jnp.stack([first_choice, second_choice], axis=1).astype(jnp.int32)
    ordered = jnp.transpose(expert_ids.reshape(blocks, TOK_DEV, 2), (0, 2, 1)).reshape(blocks, 2 * TOK_DEV)
    hits = (ordered[:, :, None] == jnp.arange(EXPERTS, dtype=jnp.int32)[None, None, :]).astype(jnp.int32)
    before = jnp.cumsum(hits, axis=1) - hits
    position = jnp.sum(before * hits, axis=2)
    position = jnp.transpose(position.reshape(blocks, 2, TOK_DEV), (0, 2, 1)).reshape(TOKENS, 2)
    slot_ids = jnp.where(position < CAP, position, -1).astype(jnp.int32)
    return (expert_ids, slot_ids)


def draw_route_expert(key, part):
    return route_pair(key)[0]


def draw_route_slot(key, part):
    return route_pair(key)[1]


def draw_qkv_weight(key, part):
    base = jnp.clip(jax.random.normal(key, (D, 3 * H * DH), jnp.float32), -6.0, 6.0) * D ** (-0.5)
    return jnp.clip(base, -3.0, 3.0).astype(jnp.bfloat16)


def draw_router_weight(key, part):
    base = jnp.clip(jax.random.normal(key, (D, EXPERTS), jnp.float32), -6.0, 6.0) * D ** (-0.5)
    return jnp.clip(base, -8.0, 8.0).astype(jnp.bfloat16)


def shard_levels(own_key, shape, cuts, low, high):
    loudness = 1.0
    for dim, blocks in cuts:
        draws = jax.random.uniform(jax.random.fold_in(jax.random.fold_in(own_key, 6), dim), (blocks,), jnp.float32, low / len(cuts), high / len(cuts))
        loudness = loudness * jnp.repeat(jnp.exp(draws), shape[dim] // blocks).reshape((-1,) + (1,) * (len(shape) - 1 - dim))
    return loudness


def bell_draw(stream_key, shape, width, limit, pieces=(), held_as=jnp.bfloat16):
    result = width * jax.random.normal(stream_key, shape, jnp.float32)
    if pieces:
        result = result * shard_levels(stream_key, shape, pieces, -0.22, 0.18)
    return jnp.clip(result, -limit, limit).astype(held_as)


def setup_inputs(seed: int = 0) -> dict:
    streams_of = jax.random.split(jax.random.key(seed), 17)
    return {
        "tokens": bell_draw(streams_of[0], (TOKENS, D), 1.0, 6.0, ((0, 8),)),
        "norm1_gain": jnp.clip(1.0 + 0.1 * jax.random.normal(streams_of[1], (D,), jnp.float32), 0.5, 1.5),
        "norm1_shift": bell_draw(streams_of[2], (D,), 0.3, 4.0, (), jnp.float32),
        "qkv_weight": draw_qkv_weight(jax.random.fold_in(streams_of[16], 71), 0),
        "proj_weight": bell_draw(streams_of[4], (H * DH, D), (H * DH // 64) ** -0.5, 1.75, ((0, 4),)),
        "proj_shift": bell_draw(streams_of[5], (D,), 1.0, 6.0, (), jnp.float32),
        "norm2_gain": jnp.clip(1.0 + 0.1 * jax.random.normal(streams_of[6], (D,), jnp.float32), 0.5, 1.5),
        "norm2_shift": bell_draw(streams_of[7], (D,), 0.3, 4.0, (), jnp.float32),
        "router_weight": draw_router_weight(jax.random.fold_in(streams_of[16], 71), 0),
        "expand_weight": bell_draw(streams_of[9], (EXPERTS, D, FF), D ** -0.5, 0.21875, ((0, 8), (2, 4))),
        "expand_shift": bell_draw(streams_of[10], (EXPERTS, FF), 0.5, 6.0, ((0, 8), (1, 4)), jnp.float32),
        "shrink_weight": bell_draw(streams_of[11], (EXPERTS, FF, D), FF ** -0.5, 0.109375, ((0, 8), (1, 4))),
        "shrink_shift": bell_draw(streams_of[12], (EXPERTS, D), 0.3, 4.0, ((0, 8),), jnp.float32),
        "route_expert": draw_route_expert(jax.random.fold_in(streams_of[16], 71), 0),
        "route_slot": draw_route_slot(jax.random.fold_in(streams_of[16], 71), 0),
        "cotangent": bell_draw(streams_of[15], (TOKENS, D), 1.0, 6.0, ((0, 8),)),
    }


norm_eps = 1e-06
half_root = 0.7071067811865476
gauss_peak = 0.3989422804014327

def normalize(values, norm_gain, norm_shift):
    row_mean = lax.optimization_barrier(jnp.mean(values, axis=1, keepdims=True))
    centered = values - row_mean
    variance = lax.optimization_barrier(jnp.mean(centered * centered, axis=1, keepdims=True))
    inverse = lax.rsqrt(variance + norm_eps)
    scaled = centered * inverse
    return (scaled * norm_gain + norm_shift, scaled, inverse)

def norm_back(upstream, scaled, inverse, norm_gain):
    weighted = upstream * norm_gain
    first_mean = lax.optimization_barrier(jnp.mean(weighted, axis=1, keepdims=True))
    second_mean = lax.optimization_barrier(jnp.mean(weighted * scaled, axis=1, keepdims=True))
    return inverse * (weighted - first_mean - scaled * second_mean)

def gelu_exact(preact):
    return 0.5 * preact * (1.0 + lax.erf(preact * half_root))

def gelu_slope(preact):
    return 0.5 * (1.0 + lax.erf(preact * half_root)) + preact * jnp.exp(-0.5 * preact * preact) * gauss_peak

def route_tables(route_expert, route_slot, experts, capacity):
    tok_count = route_expert.shape[0]
    kept = route_slot >= 0
    targets = jnp.where(kept, route_expert * capacity + route_slot, experts * capacity).reshape(-1).astype(jnp.int32)
    numbers = jnp.arange(2 * tok_count, dtype=jnp.int32)
    owners = jnp.full((experts * capacity,), 2 * tok_count, jnp.int32).at[targets].set(numbers, mode='drop')
    return (targets, owners)

def attend_front(normed_b, qkv_weight, images):
    tok_count = normed_b.shape[0]
    head_count = qkv_weight.shape[1] // (3 * DH)
    projected = jnp.dot(normed_b, qkv_weight, preferred_element_type=jnp.float32).astype(jnp.bfloat16)
    projected = projected.reshape(images, SEQ, head_count, 3, DH)
    queries = projected[:, :, :, 0]
    keys_b = projected[:, :, :, 1]
    values_b = projected[:, :, :, 2]
    scores = jnp.einsum('bqhd,bkhd->bhqk', queries.astype(jnp.float32), keys_b.astype(jnp.float32)) * DH ** (-0.5)
    row_top = lax.optimization_barrier(jnp.max(scores, axis=3, keepdims=True))
    log_total = row_top + jnp.log(lax.optimization_barrier(jnp.sum(jnp.exp(scores - row_top), axis=3, keepdims=True)))
    attn_b = jnp.exp(scores - log_total).astype(jnp.bfloat16)
    context = jnp.einsum('bhqk,bkhd->bqhd', attn_b.astype(jnp.float32), values_b.astype(jnp.float32))
    context_b = context.astype(jnp.bfloat16).reshape(tok_count, head_count * DH)
    return (queries, keys_b, values_b, log_total, context_b)

def attend_back(queries, keys_b, values_b, log_total, context_b, context_grad, images):
    tok_count = context_b.shape[0]
    head_count = queries.shape[2]
    factor = DH ** (-0.5)
    scores = jnp.einsum('bqhd,bkhd->bhqk', queries.astype(jnp.float32), keys_b.astype(jnp.float32)) * factor
    attention = jnp.exp(scores - log_total)
    attn_b = attention.astype(jnp.bfloat16)
    grad_ctx = context_grad.reshape(images, SEQ, head_count, DH).astype(jnp.float32)
    context_f = context_b.reshape(images, SEQ, head_count, DH).astype(jnp.float32)
    value_grad = jnp.einsum('bhqk,bqhd->bkhd', attn_b.astype(jnp.float32), grad_ctx)
    attn_grad = jnp.einsum('bqhd,bkhd->bhqk', grad_ctx, values_b.astype(jnp.float32))
    row_dot = jnp.transpose(lax.optimization_barrier(jnp.sum(grad_ctx * context_f, axis=3)), (0, 2, 1))[:, :, :, None]
    score_grad = (attention * (attn_grad - row_dot) * factor).astype(jnp.bfloat16).astype(jnp.float32)
    query_grad = jnp.einsum('bhqk,bkhd->bqhd', score_grad, keys_b.astype(jnp.float32))
    key_grad = jnp.einsum('bhqk,bqhd->bkhd', score_grad, queries.astype(jnp.float32))
    stacked = jnp.stack([query_grad, key_grad, value_grad], axis=3)
    return stacked.astype(jnp.bfloat16).reshape(tok_count, head_count * 3 * DH)

def quarter_sum(left_b, right_b):
    span_cols = left_b.shape[1] // N_TENSOR
    summed = jnp.zeros((left_b.shape[0], right_b.shape[1]), jnp.float32)
    for quarter in range(N_TENSOR):
        partial_value = jnp.dot(left_b[:, quarter * span_cols:(quarter + 1) * span_cols], right_b[quarter * span_cols:(quarter + 1) * span_cols], preferred_element_type=jnp.float32)
        summed = summed + lax.optimization_barrier(partial_value.astype(jnp.bfloat16)).astype(jnp.float32)
    return summed

def reference(tokens, norm1_gain, norm1_shift, qkv_weight, proj_weight, proj_shift, norm2_gain, norm2_shift, router_weight, expand_weight, expand_shift, shrink_weight, shrink_shift, route_expert, route_slot, cotangent):
    blocks = TOKENS // TOK_DEV
    tok_blocks = tokens.reshape(blocks, TOK_DEV, D)
    exp_blocks = route_expert.reshape(blocks, TOK_DEV, 2)
    slot_blocks = route_slot.reshape(blocks, TOK_DEV, 2)
    cot_blocks = cotangent.reshape(blocks, TOK_DEV, D)

    def front(token_blk, expert_blk, slot_blk):
        token_f = token_blk.astype(jnp.float32)
        normed, scaled1, inverse1 = normalize(token_f, norm1_gain, norm1_shift)
        normed_b = normed.astype(jnp.bfloat16)
        queries, keys_b, values_b, log_total, context_b = attend_front(normed_b, qkv_weight, IMG_DEV)
        hidden = token_f + jnp.dot(context_b, proj_weight, preferred_element_type=jnp.float32) + proj_shift
        normed2, scaled2, inverse2 = normalize(hidden, norm2_gain, norm2_shift)
        mixed_b = normed2.astype(jnp.bfloat16)
        logits = jnp.dot(mixed_b, router_weight, preferred_element_type=jnp.float32)
        pick_mask = (lax.broadcasted_iota(jnp.int32, (TOK_DEV, 2, EXPERTS), 2) == expert_blk[:, :, None]).astype(jnp.float32)
        chosen = lax.optimization_barrier(jnp.sum(logits[:, None, :] * pick_mask, axis=2))
        gate_top = lax.optimization_barrier(jnp.max(chosen, axis=1, keepdims=True))
        lifted = jnp.exp(chosen - gate_top)
        gate_weights = lifted / lax.optimization_barrier(jnp.sum(lifted, axis=1, keepdims=True))
        targets, owners = route_tables(expert_blk, slot_blk, EXPERTS, CAP)
        return (token_f, scaled1, inverse1, normed_b, queries, keys_b, values_b, log_total, context_b, hidden, scaled2, inverse2, mixed_b, pick_mask, gate_weights, targets, owners)

    def to_experts(stacked):
        return jnp.transpose(stacked.reshape(blocks, EXPERTS, CAP, D), (1, 0, 2, 3)).reshape(EXPERTS, blocks * CAP, D)

    def from_experts(stacked):
        return jnp.transpose(stacked.reshape(EXPERTS, blocks, CAP, D), (1, 0, 2, 3)).reshape(blocks, EXPERTS * CAP, D)

    def gather_rows(inputs):
        state = front(inputs[0], inputs[1], inputs[2])
        return jnp.take(state[12], state[16] // 2, axis=0, mode='fill', fill_value=0)
    buffers = lax.map(gather_rows, (tok_blocks, exp_blocks, slot_blocks))
    expert_rows = to_experts(buffers)

    def expert_front(inputs):
        rows_e, expand_e, eshift_e, shrink_e, sshift_e = inputs
        preact = jnp.dot(rows_e, expand_e, preferred_element_type=jnp.float32) + eshift_e
        activ_b = gelu_exact(preact).astype(jnp.bfloat16)
        return (quarter_sum(activ_b, shrink_e) + sshift_e).astype(jnp.bfloat16)
    expert_out = lax.map(expert_front, (expert_rows, expand_weight, expand_shift, shrink_weight, shrink_shift))
    returned = from_experts(expert_out)

    def middle(inputs):
        token_blk, expert_blk, slot_blk, returned_blk, cot_blk = inputs
        state = front(token_blk, expert_blk, slot_blk)
        hidden = state[9]
        gate_weights = state[14]
        picked = jnp.take(returned_blk, state[15], axis=0, mode='fill', fill_value=0).reshape(TOK_DEV, 2, D).astype(jnp.float32)
        output_blk = hidden + lax.optimization_barrier(jnp.sum(gate_weights[:, :, None] * picked, axis=1))
        weighted = (gate_weights[:, :, None] * cot_blk.astype(jnp.float32)[:, None, :]).astype(jnp.bfloat16).reshape(2 * TOK_DEV, D)
        grad_buf = jnp.take(weighted, state[16], axis=0, mode='fill', fill_value=0)
        return (output_blk, grad_buf)
    output_blocks, grad_buffers = lax.map(middle, (tok_blocks, exp_blocks, slot_blocks, returned, cot_blocks))
    slot_grad = to_experts(grad_buffers)

    def expert_back(inputs):
        rows_e, grad_e, expand_e, eshift_e, shrink_e = inputs
        preact = jnp.dot(rows_e, expand_e, preferred_element_type=jnp.float32) + eshift_e
        activ_b = gelu_exact(preact).astype(jnp.bfloat16)
        shrink_g = jnp.dot(activ_b.T, grad_e, preferred_element_type=jnp.float32)
        sshift_g = lax.optimization_barrier(jnp.sum(grad_e.astype(jnp.float32), axis=0))
        pre_grad = jnp.dot(grad_e, shrink_e.T, preferred_element_type=jnp.float32) * gelu_slope(preact)
        pre_gradb = pre_grad.astype(jnp.bfloat16)
        expand_g = jnp.dot(rows_e.T, pre_gradb, preferred_element_type=jnp.float32)
        eshift_g = lax.optimization_barrier(jnp.sum(pre_grad, axis=0))
        rows_grad = quarter_sum(pre_gradb, expand_e.T).astype(jnp.bfloat16)
        return (rows_grad, expand_g, eshift_g, shrink_g, sshift_g)
    rows_grad, expand_grad, eshift_grad, shrink_grad, sshift_grad = lax.map(expert_back, (expert_rows, slot_grad, expand_weight, expand_shift, shrink_weight))
    back_rows = from_experts(rows_grad)

    def backward_block(running, inputs):
        token_blk, expert_blk, slot_blk, returned_blk, back_blk, cot_blk = inputs
        token_f, scaled1, inverse1, normed_b, queries, keys_b, values_b, log_total, context_b, hidden, scaled2, inverse2, mixed_b, pick_mask, gate_weights, targets, owners = front(token_blk, expert_blk, slot_blk)
        upstream = cot_blk.astype(jnp.float32)
        picked = jnp.take(returned_blk, targets, axis=0, mode='fill', fill_value=0).reshape(TOK_DEV, 2, D).astype(jnp.float32)
        gate_grad = lax.optimization_barrier(jnp.sum(upstream[:, None, :] * picked, axis=2))
        common = lax.optimization_barrier(jnp.sum(gate_weights * gate_grad, axis=1, keepdims=True))
        chosen_grad = gate_weights * (gate_grad - common)
        logit_grad = lax.optimization_barrier(jnp.sum(pick_mask * chosen_grad[:, :, None], axis=1)).astype(jnp.bfloat16)
        router_g = jnp.dot(mixed_b.T, logit_grad, preferred_element_type=jnp.float32)
        back_pick = jnp.take(back_blk, targets, axis=0, mode='fill', fill_value=0).reshape(TOK_DEV, 2, D).astype(jnp.float32)
        mixed_grad = lax.optimization_barrier(jnp.sum(back_pick, axis=1)) + jnp.dot(logit_grad, router_weight.T, preferred_element_type=jnp.float32)
        gain2_g = lax.optimization_barrier(jnp.sum(mixed_grad * scaled2, axis=0))
        shift2_g = lax.optimization_barrier(jnp.sum(mixed_grad, axis=0))
        hidden_grad = upstream + norm_back(mixed_grad, scaled2, inverse2, norm2_gain)
        pshift_g = lax.optimization_barrier(jnp.sum(hidden_grad, axis=0))
        hidden_gradb = hidden_grad.astype(jnp.bfloat16)
        proj_g = jnp.dot(context_b.T, hidden_gradb, preferred_element_type=jnp.float32)
        context_grad = jnp.dot(hidden_gradb, proj_weight.T, preferred_element_type=jnp.float32).astype(jnp.bfloat16)
        qkv_gradb = attend_back(queries, keys_b, values_b, log_total, context_b, context_grad, IMG_DEV)
        qkv_g = jnp.dot(normed_b.T, qkv_gradb, preferred_element_type=jnp.float32)
        normed_grad = jnp.dot(qkv_gradb, qkv_weight.T, preferred_element_type=jnp.float32)
        gain1_g = lax.optimization_barrier(jnp.sum(normed_grad * scaled1, axis=0))
        shift1_g = lax.optimization_barrier(jnp.sum(normed_grad, axis=0))
        tokens_g = hidden_grad + norm_back(normed_grad, scaled1, inverse1, norm1_gain)
        terms = (gain1_g, shift1_g, qkv_g, proj_g, pshift_g, gain2_g, shift2_g, router_g)
        return (jax.tree.map(jnp.add, running, terms), tokens_g)
    zero_width = jnp.zeros((D,), jnp.float32)
    initial = (zero_width, zero_width, jnp.zeros((D, 3 * H * DH), jnp.float32), jnp.zeros((H * DH, D), jnp.float32), zero_width, zero_width, zero_width, jnp.zeros((D, EXPERTS), jnp.float32))
    running, tokens_blocks = lax.scan(backward_block, initial, (tok_blocks, exp_blocks, slot_blocks, returned, back_rows, cot_blocks))
    return (output_blocks.reshape(TOKENS, D), tokens_blocks.reshape(TOKENS, D), running[0], running[1], running[2], running[3], running[4], running[5], running[6], running[7], expand_grad, eshift_grad, shrink_grad, sshift_grad)
```

```python
import jax
import jax.numpy as jnp
from jax import lax
from jax.experimental import pallas as pl
from jax.experimental.pallas import tpu as pltpu
from jax.sharding import PartitionSpec as P

DH = 64
SEQ = 197


norm_eps = 1e-06
half_root = 0.7071067811865476
gauss_peak = 0.3989422804014327


def normalize(values, norm_gain, norm_shift):
    row_mean = jnp.mean(values, axis=1, keepdims=True)
    centered = values - row_mean
    variance = jnp.mean(centered * centered, axis=1, keepdims=True)
    inverse = lax.rsqrt(variance + norm_eps)
    scaled = centered * inverse
    return (scaled * norm_gain + norm_shift, scaled, inverse)


def norm_back(upstream, scaled, inverse, norm_gain):
    weighted = upstream * norm_gain
    first_mean = jnp.mean(weighted, axis=1, keepdims=True)
    second_mean = jnp.mean(weighted * scaled, axis=1, keepdims=True)
    return inverse * (weighted - first_mean - scaled * second_mean)


def gelu_exact(preact):
    return 0.5 * preact * (1.0 + lax.erf(preact * half_root))


def gelu_slope(preact):
    return (
        0.5 * (1.0 + lax.erf(preact * half_root))
        + preact * jnp.exp(-0.5 * preact * preact) * gauss_peak
    )


def inner_rows(left_b, right_b):
    return lax.dot_general(
        left_b, right_b, (((0,), (0,)), ((), ())), preferred_element_type=jnp.float32
    )


def outer_cols(left_b, right_b):
    return lax.dot_general(
        left_b, right_b, (((1,), (1,)), ((), ())), preferred_element_type=jnp.float32
    )


def route_tables(route_expert, route_slot, experts, capacity):
    tok_count = route_expert.shape[0]
    kept = route_slot >= 0
    targets = jnp.where(kept, route_expert * capacity + route_slot, experts * capacity).reshape(-1)
    numbers = jnp.arange(2 * tok_count, dtype=jnp.int32)
    owners = (
        jnp.full((experts * capacity,), 2 * tok_count, jnp.int32)
        .at[targets]
        .set(numbers, mode="drop")
    )
    return (targets, owners)


def heads_total(partial_value):
    return lax.psum(partial_value.astype(jnp.bfloat16), "tensor").astype(jnp.float32)


def send_rows(buffer):
    return lax.all_to_all(buffer, "expert", split_axis=0, concat_axis=0, tiled=True)


def return_rows(partial_value, offset):
    summed = lax.psum(partial_value.astype(jnp.bfloat16), "tensor").astype(jnp.float32)
    ready = (summed + offset).astype(jnp.bfloat16)
    return lax.all_to_all(ready, "expert", split_axis=0, concat_axis=0, tiled=True)


def attend_front(normed_b, qkv_weight, images):
    tok_count = normed_b.shape[0]
    head_count = qkv_weight.shape[1] // (3 * DH)
    projected = jnp.dot(normed_b, qkv_weight, preferred_element_type=jnp.float32).astype(
        jnp.bfloat16
    )
    projected = projected.reshape(images, SEQ, head_count, 3, DH)
    queries = projected[:, :, :, 0]
    keys_b = projected[:, :, :, 1]
    values_b = projected[:, :, :, 2]
    scores = jnp.einsum(
        "bqhd,bkhd->bhqk", queries, keys_b, preferred_element_type=jnp.float32
    ) * DH ** (-0.5)
    row_top = jnp.max(scores, axis=3, keepdims=True)
    log_total = row_top + jnp.log(jnp.sum(jnp.exp(scores - row_top), axis=3, keepdims=True))
    attn_b = jnp.exp(scores - log_total).astype(jnp.bfloat16)
    context = jnp.einsum("bhqk,bkhd->bqhd", attn_b, values_b, preferred_element_type=jnp.float32)
    context_b = context.astype(jnp.bfloat16).reshape(tok_count, head_count * DH)
    return (queries, keys_b, values_b, log_total, context_b)


def attend_back(queries, keys_b, values_b, log_total, context_b, context_grad, images):
    tok_count = context_b.shape[0]
    head_count = queries.shape[2]
    factor = DH ** (-0.5)
    scores = (
        jnp.einsum("bqhd,bkhd->bhqk", queries, keys_b, preferred_element_type=jnp.float32) * factor
    )
    attention = jnp.exp(scores - log_total)
    attn_b = attention.astype(jnp.bfloat16)
    grad_ctx = context_grad.reshape(images, SEQ, head_count, DH)
    context_four = context_b.reshape(images, SEQ, head_count, DH)
    value_grad = jnp.einsum("bhqk,bqhd->bkhd", attn_b, grad_ctx, preferred_element_type=jnp.float32)
    attn_grad = jnp.einsum(
        "bqhd,bkhd->bhqk", grad_ctx, values_b, preferred_element_type=jnp.float32
    )
    row_dot = jnp.sum(grad_ctx.astype(jnp.float32) * context_four.astype(jnp.float32), axis=3)
    row_dot = jnp.transpose(row_dot, (0, 2, 1))[:, :, :, None]
    score_grad = (attention * (attn_grad - row_dot) * factor).astype(jnp.bfloat16)
    query_grad = jnp.einsum(
        "bhqk,bkhd->bqhd", score_grad, keys_b, preferred_element_type=jnp.float32
    )
    key_grad = jnp.einsum(
        "bhqk,bqhd->bkhd", score_grad, queries, preferred_element_type=jnp.float32
    )
    stacked = jnp.stack([query_grad, key_grad, value_grad], axis=3)
    return stacked.astype(jnp.bfloat16).reshape(tok_count, head_count * 3 * DH)


def plain_device(
    tokens,
    norm1_gain,
    norm1_shift,
    qkv_weight,
    proj_weight,
    proj_shift,
    norm2_gain,
    norm2_shift,
    router_weight,
    expand_weight,
    expand_shift,
    shrink_weight,
    shrink_shift,
    route_expert,
    route_slot,
    cotangent,
):
    experts = lax.axis_size("expert")
    tensor_count = lax.axis_size("tensor")
    tok_count = tokens.shape[0]
    images = tok_count // SEQ
    capacity = tensor_count * (5 * tok_count // (2 * experts * tensor_count) + 1)
    width = tokens.shape[1]
    token_f = tokens.astype(jnp.float32)
    normed, scaled1, inverse1 = normalize(token_f, norm1_gain, norm1_shift)
    normed_b = normed.astype(jnp.bfloat16)
    queries, keys_b, values_b, log_total, context_b = attend_front(normed_b, qkv_weight, images)
    attn_part = jnp.dot(context_b, proj_weight, preferred_element_type=jnp.float32)
    hidden = token_f + heads_total(attn_part) + proj_shift
    normed2, scaled2, inverse2 = normalize(hidden, norm2_gain, norm2_shift)
    mixed_b = normed2.astype(jnp.bfloat16)
    logits = jnp.dot(mixed_b, router_weight, preferred_element_type=jnp.float32)
    pick_mask = (
        lax.broadcasted_iota(jnp.int32, (tok_count, 2, experts), 2) == route_expert[:, :, None]
    ).astype(jnp.float32)
    chosen = jnp.sum(logits[:, None, :] * pick_mask, axis=2)
    gate_top = jnp.max(chosen, axis=1, keepdims=True)
    lifted = jnp.exp(chosen - gate_top)
    gate_weights = lifted / jnp.sum(lifted, axis=1, keepdims=True)
    targets, owners = route_tables(route_expert, route_slot, experts, capacity)
    buffer = jnp.take(mixed_b, owners // 2, axis=0, mode="fill", fill_value=0).reshape(
        experts, capacity, width
    )
    received = send_rows(buffer).reshape(experts * capacity, width)
    preact = (
        jnp.dot(received, expand_weight[0], preferred_element_type=jnp.float32) + expand_shift[0]
    )
    activ_b = gelu_exact(preact).astype(jnp.bfloat16)
    out_part = jnp.dot(activ_b, shrink_weight[0], preferred_element_type=jnp.float32).reshape(
        experts, capacity, width
    )
    returned = return_rows(out_part, shrink_shift[0]).reshape(experts * capacity, width)
    picked = (
        jnp.take(returned, targets, axis=0, mode="fill", fill_value=0)
        .reshape(tok_count, 2, width)
        .astype(jnp.float32)
    )
    output = hidden + jnp.sum(gate_weights[:, :, None] * picked, axis=1)
    upstream = cotangent.astype(jnp.float32)
    gate_grad = jnp.sum(upstream[:, None, :] * picked, axis=2)
    weighted = (
        (gate_weights[:, :, None] * upstream[:, None, :])
        .astype(jnp.bfloat16)
        .reshape(2 * tok_count, width)
    )
    grad_buffer = jnp.take(weighted, owners, axis=0, mode="fill", fill_value=0).reshape(
        experts, capacity, width
    )
    grad_recv = send_rows(grad_buffer).reshape(experts * capacity, width)
    shrink_g = inner_rows(activ_b, grad_recv)
    sshift_g = jnp.sum(grad_recv.astype(jnp.float32), axis=0)
    pre_grad = outer_cols(grad_recv, shrink_weight[0]) * gelu_slope(preact)
    pre_gradb = pre_grad.astype(jnp.bfloat16)
    expand_g = inner_rows(received, pre_gradb)
    eshift_g = jnp.sum(pre_grad, axis=0)
    rows_part = outer_cols(pre_gradb, expand_weight[0]).reshape(experts, capacity, width)
    back_rows = return_rows(rows_part, 0.0).reshape(experts * capacity, width)
    common = jnp.sum(gate_weights * gate_grad, axis=1, keepdims=True)
    chosen_grad = gate_weights * (gate_grad - common)
    logit_grad = jnp.sum(pick_mask * chosen_grad[:, :, None], axis=1).astype(jnp.bfloat16)
    router_g = inner_rows(mixed_b, logit_grad)
    back_pick = (
        jnp.take(back_rows, targets, axis=0, mode="fill", fill_value=0)
        .reshape(tok_count, 2, width)
        .astype(jnp.float32)
    )
    mixed_grad = jnp.sum(back_pick, axis=1) + outer_cols(logit_grad, router_weight)
    gain2_g = jnp.sum(mixed_grad * scaled2, axis=0)
    shift2_g = jnp.sum(mixed_grad, axis=0)
    hidden_grad = upstream + norm_back(mixed_grad, scaled2, inverse2, norm2_gain)
    pshift_g = jnp.sum(hidden_grad, axis=0)
    hidden_gradb = hidden_grad.astype(jnp.bfloat16)
    proj_g = inner_rows(context_b, hidden_gradb)
    context_grad = outer_cols(hidden_gradb, proj_weight).astype(jnp.bfloat16)
    qkv_gradb = attend_back(queries, keys_b, values_b, log_total, context_b, context_grad, images)
    qkv_g = inner_rows(normed_b, qkv_gradb)
    normed_grad = heads_total(outer_cols(qkv_gradb, qkv_weight))
    gain1_g = jnp.sum(normed_grad * scaled1, axis=0)
    shift1_g = jnp.sum(normed_grad, axis=0)
    tokens_grad = hidden_grad + norm_back(normed_grad, scaled1, inverse1, norm1_gain)
    summed = lax.psum(
        (gain1_g, shift1_g, qkv_g, proj_g, pshift_g, gain2_g, shift2_g, router_g), "expert"
    )
    return (
        output,
        tokens_grad,
        summed[0],
        summed[1],
        summed[2],
        summed[3],
        summed[4],
        summed[5],
        summed[6],
        summed[7],
        expand_g[None],
        eshift_g[None],
        shrink_g[None],
        sshift_g[None],
    )

MESH = pl.DeviceIdType.MESH
F32 = jnp.float32
BF16 = jnp.bfloat16


def place():
    e = lax.axis_index("expert")
    t = lax.axis_index("tensor")
    a = t // 2
    c = t % 2
    return e, t, a, c, (e, 2 * a + 1 - c), (e, 2 * (1 - a) + c)


def greet(devices):
    barrier = pltpu.get_barrier_semaphore()
    for device in devices:
        pl.semaphore_signal(barrier, inc=1, device_id=device, device_id_type=MESH)
    pl.semaphore_wait(barrier, len(devices))


def remote(src, dst, send, recv, device):
    return pltpu.make_async_remote_copy(
        src_ref=src, dst_ref=dst, send_sem=send, recv_sem=recv, device_id=device, device_id_type=MESH
    )


def lanes(index, width):
    return pl.ds(pl.multiple_of(index * width, 128), width)


def call(kernel, outs, scratch, number, args):
    vmem = pl.BlockSpec(memory_space=pltpu.VMEM)
    return pl.pallas_call(
        kernel,
        out_shape=outs,
        in_specs=[vmem] * len(args),
        out_specs=jax.tree.map(lambda _: vmem, outs),
        scratch_shapes=scratch,
        compiler_params=pltpu.CompilerParams(
            collective_id=number, has_side_effects=True, vmem_limit_bytes=48 * 1024 * 1024
        ),
    )(*args)


def tensor_sum_kernel(x, out, got1, part, got2, send, recv):
    e, t, a, c, core, across = place()
    greet([core, across])
    half = x.shape[1] // 2
    mine, other = lanes(c, half), lanes(1 - c, half)
    copy = remote(x.at[:, other], got1, send.at[0], recv.at[0], core)
    copy.start()
    copy.wait()
    part[...] = (x[:, mine].astype(F32) + got1[...].astype(F32)).astype(BF16)
    copy = remote(part, got2, send.at[1], recv.at[1], across)
    copy.start()
    copy.wait()
    out[:, mine] = (part[...].astype(F32) + got2[...].astype(F32)).astype(BF16)
    copy = remote(out.at[:, mine], out.at[:, mine], send.at[2], recv.at[2], core)
    copy.start()
    copy.wait()


def tensor_sum(x, number):
    rows, width = x.shape
    half = pltpu.VMEM((rows, width // 2), BF16)
    sems = pltpu.SemaphoreType.DMA((3,))
    return call(
        tensor_sum_kernel,
        jax.ShapeDtypeStruct((rows, width), BF16),
        [half, half, half, sems, sems],
        number,
        (x,),
    )


def dispatch_kernel(first, second, out0, out1, send_far, send_across, send_core, recv, local):
    e, t, a, c, core, across = place()
    count = first.shape[0]
    peers = [(lax.rem(e + d, count), t) for d in range(1, count)]
    greet(peers + [core, across])
    ins, outs = (first, second), (out0, out1)
    sent = []

    def push(src, k, origin, quarter, send, device):
        copy = remote(src, outs[k].at[origin, quarter], send, recv.at[k, origin, quarter], device)
        copy.start()
        sent.append(copy)

    def arrive(k, origin, quarter):
        spot = outs[k].at[origin, quarter]
        remote(spot, spot, send_core.at[k, origin, quarter], recv.at[k, origin, quarter], core).wait_recv()

    for d in range(1, count):
        dst = lax.rem(e + d, count)
        for k in range(2):
            push(ins[k].at[dst], k, e, t, send_far.at[k, d], (dst, t))
    keeps = []
    for k in range(2):
        push(ins[k].at[e], k, e, t, send_across.at[k, e], across)
        push(ins[k].at[e], k, e, t, send_core.at[k, e, t], core)
        keep = pltpu.make_async_copy(ins[k].at[e], outs[k].at[e, t], local.at[k])
        keep.start()
        keeps.append(keep)
    far = 2 * (1 - a) + c
    for d in range(1, count + 1):
        if d < count:
            origin = lax.rem(e - d + count, count)
            for k in range(2):
                arrive(k, origin, t)
                push(outs[k].at[origin, t], k, origin, t, send_across.at[k, origin], across)
                push(outs[k].at[origin, t], k, origin, t, send_core.at[k, origin, t], core)
        origin = lax.rem(e - d + 1 + count, count)
        for k in range(2):
            arrive(k, origin, far)
            push(outs[k].at[origin, far], k, origin, far, send_core.at[k, origin, far], core)
    for d in range(count):
        origin = lax.rem(e - d + count, count)
        for k in range(2):
            arrive(k, origin, 2 * a + 1 - c)
            arrive(k, origin, 2 * (1 - a) + 1 - c)
    for copy in sent:
        copy.wait_send()
    for keep in keeps:
        keep.wait()


def dispatch(first, second, number):
    count, rows, width = first.shape
    out = jax.ShapeDtypeStruct((count, 4, rows, width), BF16)
    dma = pltpu.SemaphoreType.DMA
    return call(
        dispatch_kernel,
        (out, out),
        [dma((2, count)), dma((2, count)), dma((2, count, 4)), dma((2, count, 4)), dma((2,))],
        number,
        (first, second),
    )


def collect_kernel(
    part0, part1, shift, out0, out1, got1, half1, got2, ready,
    send1, recv1, send2, recv2, send3, recv3, send4, recv4, local,
):
    e, t, a, c, core, across = place()
    count = part0.shape[0]
    peers = [(lax.rem(e + d, count), t) for d in range(1, count)]
    greet(peers + [core, across])
    parts, outs = (part0, part1), (out0, out1)
    rows = part0.shape[1] // 2
    width = part0.shape[2] // 2
    mine, other = pl.ds(c * rows, rows), pl.ds((1 - c) * rows, rows)
    left, right = lanes(a, width), lanes(1 - a, width)
    order = [lax.rem(e + d, count) for d in range(1, count + 1)]
    steps = [(dst, k) for dst in order for k in range(2)]
    stage1, stage2, rest = [], [], []
    for dst, k in steps:
        copy = remote(parts[k].at[dst, other], got1.at[k, dst], send1.at[k, dst], recv1.at[k, dst], core)
        copy.start()
        stage1.append(copy)
    for i, (dst, k) in enumerate(steps):
        stage1[i].wait_recv()
        half1[k, dst] = (parts[k][dst, mine].astype(F32) + got1[k, dst].astype(F32)).astype(BF16)
        copy = remote(
            half1.at[k, dst, :, right], got2.at[k, dst], send2.at[k, dst], recv2.at[k, dst], across
        )
        copy.start()
        stage2.append(copy)
    keeps = []
    for i, (dst, k) in enumerate(steps):
        stage2[i].wait_recv()
        total = half1[k, dst, :, left].astype(F32) + got2[k, dst].astype(F32)
        if k == 0:
            total = total + shift[:, left]
        ready[k, dst] = total.astype(BF16)
        if i < len(steps) - 2:
            copy = remote(ready.at[k, dst], outs[k].at[e, c], send3.at[k, dst], recv3.at[k, e], (dst, t))
            copy.start()
            rest.append(copy)
        else:
            copy = remote(ready.at[k, dst], outs[k].at[e, c], send4.at[k, e], recv4.at[k, e], core)
            copy.start()
            rest.append(copy)
            keep = pltpu.make_async_copy(ready.at[k, dst], outs[k].at[e, c], local.at[k])
            keep.start()
            keeps.append(keep)
    for d in range(1, count):
        origin = lax.rem(e - d + count, count)
        for k in range(2):
            spot = outs[k].at[origin, c]
            remote(spot, spot, send4.at[k, origin], recv3.at[k, origin], core).wait_recv()
            copy = remote(spot, spot, send4.at[k, origin], recv4.at[k, origin], core)
            copy.start()
            rest.append(copy)
    for d in range(count):
        origin = lax.rem(e - d + count, count)
        for k in range(2):
            spot = outs[k].at[origin, 1 - c]
            remote(spot, spot, send4.at[k, origin], recv4.at[k, origin], core).wait_recv()
    for copy in stage1 + stage2 + rest:
        copy.wait_send()
    for keep in keeps:
        keep.wait()


def collect(part0, part1, shift, number):
    count, rows, width = part0.shape
    out = jax.ShapeDtypeStruct((count, 2, rows // 2, width // 2), BF16)
    dma = pltpu.SemaphoreType.DMA
    full = pltpu.VMEM((2, count, rows // 2, width), BF16)
    half = pltpu.VMEM((2, count, rows // 2, width // 2), BF16)
    return call(
        collect_kernel,
        (out, out),
        [full, full, half, half] + [dma((2, count))] * 8 + [dma((2,))],
        number,
        (part0, part1, shift),
    )


def swap_kernel(first, second, gate, out0, out1, gate_out, got, send, recv, send_gate, recv_gate):
    e, t, a, c, core, across = place()
    greet([core, across])
    width = first.shape[1]
    mine, other = lanes(a, width), lanes(1 - a, width)
    small = remote(gate, got, send_gate, recv_gate, across)
    small.start()

    def trade(src, out, out_other):
        out_here = out.at[:, mine]
        copy = remote(src, out_here, send.at[0], recv.at[0], across)
        copy.start()
        out0[:, mine] = first[...]
        out1[:, mine] = second[...]
        copy.wait()
        spot = out.at[:, other]
        copy = remote(spot, spot, send.at[1], recv.at[1], core)
        copy.start()
        spot_other = out_other.at[:, other]
        remote(spot_other, spot_other, send.at[1], recv.at[1], core).wait_recv()
        copy.wait_send()

    @pl.when(c == 0)
    def _():
        trade(first, out0, out1)

    @pl.when(c == 1)
    def _():
        trade(second, out1, out0)

    small.wait()
    gate_out[...] = gate[...] + got[...]


def swap(first, second, gate, number):
    rows, width = first.shape
    out = jax.ShapeDtypeStruct((rows, 2 * width), BF16)
    dma = pltpu.SemaphoreType.DMA
    return call(
        swap_kernel,
        (out, out, jax.ShapeDtypeStruct(gate.shape, F32)),
        [pltpu.VMEM(gate.shape, F32), dma((2,)), dma((2,)), dma(()), dma(())],
        number,
        (first, second, gate),
    )


def expert_sum_kernel(
    big, small, out, out_small, got1, sgot1, half1, shalf1, got2, sgot2,
    send1, recv1, send2, recv2, send3, recv3, send4, recv4,
):
    e, t, a, c, core, across = place()
    z = e // 2
    y = e % 2
    deep = big.shape[0] // 2
    beside = (2 * z + 1 - y, t)
    greet([beside] + [(2 * lax.rem(z + d, deep) + y, t) for d in range(1, deep)])
    stage1, stage2, rest = [], [], []
    order = [2, 1, 3, 0]
    for d in order:
        zz = lax.rem(z + d, deep)
        chunk = 2 * zz + 1 - y
        pair = (
            remote(big.at[chunk], got1.at[zz], send1.at[0, zz], recv1.at[0, zz], beside),
            remote(small.at[chunk], sgot1.at[zz], send1.at[1, zz], recv1.at[1, zz], beside),
        )
        for copy in pair:
            copy.start()
        stage1.append(pair)
    for i, d in enumerate(order):
        zz = lax.rem(z + d, deep)
        chunk = 2 * zz + y
        for copy in stage1[i]:
            copy.wait_recv()
        half1[zz] = (big[chunk].astype(F32) + got1[zz].astype(F32)).astype(BF16)
        shalf1[zz] = small[chunk] + sgot1[zz]
        if d:
            for copy in (
                remote(half1.at[zz], got2.at[z], send2.at[0, zz], recv2.at[0, z], (chunk, t)),
                remote(shalf1.at[zz], sgot2.at[z], send2.at[1, zz], recv2.at[1, z], (chunk, t)),
            ):
                copy.start()
                rest.append(copy)
    total = half1[z].astype(F32)
    stotal = shalf1[z]
    for d in (3, 1, 2):
        zz = lax.rem(z + d, deep)
        spot, sspot = got2.at[zz], sgot2.at[zz]
        remote(spot, spot, send2.at[0, zz], recv2.at[0, zz], beside).wait_recv()
        remote(sspot, sspot, send2.at[1, zz], recv2.at[1, zz], beside).wait_recv()
        total = total + got2[zz].astype(F32)
        stotal = stotal + sgot2[zz]
    out[e] = total.astype(BF16)
    out_small[e] = stotal
    both = (out, out_small)
    for d in (2, 1, 3):
        zz = lax.rem(z + d, deep)
        for k in range(2):
            spot = both[k].at[e]
            copy = remote(spot, spot, send3.at[k, zz], recv3.at[k, z], (2 * zz + y, t))
            copy.start()
            rest.append(copy)
    for d in (0, 3, 1, 2):
        zz = lax.rem(z + d, deep)
        for k in range(2):
            spot = both[k].at[2 * zz + y]
            if d:
                remote(spot, spot, send4.at[k, zz], recv3.at[k, zz], beside).wait_recv()
            copy = remote(spot, spot, send4.at[k, zz], recv4.at[k, zz], beside)
            copy.start()
            rest.append(copy)
    for zz in range(deep):
        for k in range(2):
            spot = both[k].at[2 * zz + 1 - y]
            remote(spot, spot, send4.at[k, zz], recv4.at[k, zz], beside).wait_recv()
    for pair in stage1:
        for copy in pair:
            copy.wait_send()
    for copy in rest:
        copy.wait_send()


def expert_sum(big, small, number):
    count, rows, width = big.shape
    deep = count // 2
    dma = pltpu.SemaphoreType.DMA
    large = pltpu.VMEM((deep, rows, width), BF16)
    little = pltpu.VMEM((deep,) + small.shape[1:], F32)
    return call(
        expert_sum_kernel,
        (jax.ShapeDtypeStruct(big.shape, BF16), jax.ShapeDtypeStruct(small.shape, F32)),
        [large, little, large, little, large, little] + [dma((2, deep))] * 8,
        number,
        (big, small),
    )


def fast_device(
    tokens,
    norm1_gain,
    norm1_shift,
    qkv_weight,
    proj_weight,
    proj_shift,
    norm2_gain,
    norm2_shift,
    router_weight,
    expand_weight,
    expand_shift,
    shrink_weight,
    shrink_shift,
    route_expert,
    route_slot,
    cotangent,
):
    experts = lax.axis_size("expert")
    tensor_count = lax.axis_size("tensor")
    tensor_index = lax.axis_index("tensor")
    tok_count = tokens.shape[0]
    images = tok_count // SEQ
    capacity = tensor_count * (5 * tok_count // (2 * experts * tensor_count) + 1)
    quarter = -(-capacity // (16 * tensor_count)) * 16
    padded = quarter * tensor_count
    width = tokens.shape[1]
    half = width // 2
    token_f = tokens.astype(F32)
    normed, scaled1, inverse1 = normalize(token_f, norm1_gain, norm1_shift)
    normed_b = normed.astype(BF16)
    queries, keys_b, values_b, log_total, context_b = attend_front(normed_b, qkv_weight, images)
    attn_part = jnp.dot(context_b, proj_weight, preferred_element_type=F32).astype(BF16)
    hidden = token_f + tensor_sum(attn_part, 1).astype(F32) + proj_shift
    normed2, scaled2, inverse2 = normalize(hidden, norm2_gain, norm2_shift)
    mixed_b = normed2.astype(BF16)
    logits = jnp.dot(mixed_b, router_weight, preferred_element_type=F32)
    picks = [
        lax.broadcasted_iota(jnp.int32, (tok_count, experts), 1) == route_expert[:, j : j + 1]
        for j in range(2)
    ]
    chosen = [jnp.sum(jnp.where(pick, logits, 0.0), axis=1, keepdims=True) for pick in picks]
    gate_top = jnp.maximum(chosen[0], chosen[1])
    lifted = [jnp.exp(value - gate_top) for value in chosen]
    gates = [value / (lifted[0] + lifted[1]) for value in lifted]
    spots = jnp.where(route_slot >= 0, route_expert * padded + route_slot, -1)
    spots_t = spots.T
    row_ids = lax.broadcasted_iota(jnp.int32, (experts, quarter, 1), 0) * padded
    row_ids = row_ids + lax.broadcasted_iota(jnp.int32, (experts, quarter, 1), 1)
    row_ids = (row_ids + tensor_index * quarter).reshape(experts * quarter, 1)
    hits = [row_ids == spots_t[j][None, :] for j in range(2)]
    chooser = (hits[0] | hits[1]).astype(BF16)
    slot_gate = jnp.sum(
        jnp.where(hits[0], gates[0].reshape(1, -1), 0.0)
        + jnp.where(hits[1], gates[1].reshape(1, -1), 0.0),
        axis=1,
        keepdims=True,
    )
    rows_out = jnp.dot(chooser, mixed_b, preferred_element_type=F32).astype(BF16)
    grad_out = (slot_gate * jnp.dot(chooser, cotangent, preferred_element_type=F32)).astype(BF16)
    received, grad_recv = dispatch(
        rows_out.reshape(experts, quarter, width), grad_out.reshape(experts, quarter, width), 2
    )
    received = received.reshape(experts * padded, width)
    grad_recv = grad_recv.reshape(experts * padded, width)
    preact = jnp.dot(received, expand_weight[0], preferred_element_type=F32) + expand_shift[0]
    activ_b = gelu_exact(preact).astype(BF16)
    out_part = jnp.dot(activ_b, shrink_weight[0], preferred_element_type=F32).astype(BF16)
    pre_grad = outer_cols(grad_recv, shrink_weight[0]) * gelu_slope(preact)
    pre_gradb = pre_grad.astype(BF16)
    rows_part = outer_cols(pre_gradb, expand_weight[0]).astype(BF16)
    returned, back_rows = collect(
        out_part.reshape(experts, padded, width),
        rows_part.reshape(experts, padded, width),
        shrink_shift,
        3,
    )
    returned = returned.reshape(experts * padded, half)
    back_rows = back_rows.reshape(experts * padded, half)
    shrink_g = inner_rows(activ_b, grad_recv)
    sshift_g = jnp.sum(grad_recv.astype(F32), axis=0)
    expand_g = inner_rows(received, pre_gradb)
    eshift_g = jnp.sum(pre_grad, axis=0)
    upstream = cotangent.astype(F32)
    slots = lax.broadcasted_iota(jnp.int32, (tok_count, experts * padded), 1)
    marks = [slots == spots[:, j : j + 1] for j in range(2)]
    mixer = (jnp.where(marks[0], gates[0], 0.0) + jnp.where(marks[1], gates[1], 0.0)).astype(BF16)
    gather = (marks[0] | marks[1]).astype(BF16)
    added = jnp.dot(mixer, returned, preferred_element_type=F32).astype(BF16)
    back = jnp.dot(gather, back_rows, preferred_element_type=F32).astype(BF16)
    cot_half = lax.dynamic_slice(cotangent, (0, (tensor_index // 2) * half), (tok_count, half))
    dots = outer_cols(cot_half, returned)
    gate_part = jnp.stack([jnp.sum(jnp.where(mark, dots, 0.0), axis=1) for mark in marks])
    gate_part = jnp.pad(gate_part, ((0, 6), (0, -tok_count % 128)))
    added, back, gate_full = swap(added, back, gate_part, 4)
    output = hidden + added.astype(F32)
    gate_grad = [gate_full[j, :tok_count].reshape(tok_count, 1) for j in range(2)]
    common = gates[0] * gate_grad[0] + gates[1] * gate_grad[1]
    logit_grad = (
        jnp.where(picks[0], gates[0] * (gate_grad[0] - common), 0.0)
        + jnp.where(picks[1], gates[1] * (gate_grad[1] - common), 0.0)
    ).astype(BF16)
    router_g = inner_rows(logit_grad, mixed_b)
    mixed_grad = back.astype(F32) + outer_cols(logit_grad, router_weight)
    gain2_g = jnp.sum(mixed_grad * scaled2, axis=0)
    shift2_g = jnp.sum(mixed_grad, axis=0)
    hidden_grad = upstream + norm_back(mixed_grad, scaled2, inverse2, norm2_gain)
    pshift_g = jnp.sum(hidden_grad, axis=0)
    hidden_gradb = hidden_grad.astype(BF16)
    context_grad = outer_cols(hidden_gradb, proj_weight).astype(BF16)
    qkv_gradb = attend_back(queries, keys_b, values_b, log_total, context_b, context_grad, images)
    normed_grad = tensor_sum(outer_cols(qkv_gradb, qkv_weight).astype(BF16), 5).astype(F32)
    gain1_g = jnp.sum(normed_grad * scaled1, axis=0)
    shift1_g = jnp.sum(normed_grad, axis=0)
    tokens_grad = hidden_grad + norm_back(normed_grad, scaled1, inverse1, norm1_gain)
    qkv_g = inner_rows(normed_b, qkv_gradb)
    proj_g = inner_rows(hidden_gradb, context_b)
    big = jnp.concatenate([qkv_g.astype(BF16), proj_g.astype(BF16)], axis=1)
    wide = big.shape[1]
    small = jnp.concatenate(
        [jnp.stack([gain1_g, shift1_g, pshift_g, gain2_g, shift2_g]), router_g], axis=0
    )
    names = small.shape[0]
    piece = width // experts
    small = jnp.pad(small, ((0, -names % 8), (0, 0)))
    small = small.reshape(small.shape[0], experts, piece).transpose(1, 0, 2)
    small = jnp.pad(small, ((0, 0), (0, 0), (0, -piece % 128)))
    big, small = expert_sum(big.reshape(experts, piece, wide), small, 6)
    big = big.reshape(width, wide)
    small = small[:, :, :piece].transpose(1, 0, 2).reshape(-1, width)
    return (
        output,
        tokens_grad,
        small[0],
        small[1],
        big[:, : qkv_g.shape[1]].astype(F32),
        big[:, qkv_g.shape[1] :].T.astype(F32),
        small[2],
        small[3],
        small[4],
        small[5:names].T,
        expand_g[None],
        eshift_g[None],
        shrink_g[None],
        sshift_g[None],
    )


def solution(mesh):
    small_mesh = mesh.shape["expert"] == 8 and mesh.shape["tensor"] == 4
    on_device = fast_device if small_mesh else plain_device
    return jax.shard_map(
        on_device,
        mesh=mesh,
        in_specs=(
            P("expert", None),
            P(),
            P(),
            P(None, "tensor"),
            P("tensor", None),
            P(),
            P(),
            P(),
            P(),
            P("expert", None, "tensor"),
            P("expert", "tensor"),
            P("expert", "tensor", None),
            P("expert", None),
            P("expert", None),
            P("expert", None),
            P("expert", None),
        ),
        out_specs=(
            P("expert", None),
            P("expert", None),
            P(),
            P(),
            P(None, "tensor"),
            P("tensor", None),
            P(),
            P(),
            P(),
            P(),
            P("expert", None, "tensor"),
            P("expert", "tensor"),
            P("expert", "tensor", None),
            P("expert", None),
        ),
        check_vma=False,
    )
```

```python
import jax
import jax.numpy as jnp
from jax import lax
from jax.experimental import pallas as pl
from jax.experimental.pallas import tpu as pltpu
from jax.sharding import PartitionSpec as P

DH = 64
SEQ = 197


norm_eps = 1e-06
half_root = 0.7071067811865476
gauss_peak = 0.3989422804014327


def normalize(values, norm_gain, norm_shift):
    row_mean = jnp.mean(values, axis=1, keepdims=True)
    centered = values - row_mean
    variance = jnp.mean(centered * centered, axis=1, keepdims=True)
    inverse = lax.rsqrt(variance + norm_eps)
    scaled = centered * inverse
    return (scaled * norm_gain + norm_shift, scaled, inverse)


def norm_back(upstream, scaled, inverse, norm_gain):
    weighted = upstream * norm_gain
    first_mean = jnp.mean(weighted, axis=1, keepdims=True)
    second_mean = jnp.mean(weighted * scaled, axis=1, keepdims=True)
    return inverse * (weighted - first_mean - scaled * second_mean)


def gelu_exact(preact):
    return 0.5 * preact * (1.0 + lax.erf(preact * half_root))


def gelu_slope(preact):
    return (
        0.5 * (1.0 + lax.erf(preact * half_root))
        + preact * jnp.exp(-0.5 * preact * preact) * gauss_peak
    )


def inner_rows(left_b, right_b):
    return lax.dot_general(
        left_b, right_b, (((0,), (0,)), ((), ())), preferred_element_type=jnp.float32
    )


def outer_cols(left_b, right_b):
    return lax.dot_general(
        left_b, right_b, (((1,), (1,)), ((), ())), preferred_element_type=jnp.float32
    )


def route_tables(route_expert, route_slot, experts, capacity):
    tok_count = route_expert.shape[0]
    kept = route_slot >= 0
    targets = jnp.where(kept, route_expert * capacity + route_slot, experts * capacity).reshape(-1)
    numbers = jnp.arange(2 * tok_count, dtype=jnp.int32)
    owners = (
        jnp.full((experts * capacity,), 2 * tok_count, jnp.int32)
        .at[targets]
        .set(numbers, mode="drop")
    )
    return (targets, owners)


def heads_total(partial_value):
    return lax.psum(partial_value.astype(jnp.bfloat16), "tensor").astype(jnp.float32)


def send_rows(buffer):
    return lax.all_to_all(buffer, "expert", split_axis=0, concat_axis=0, tiled=True)


def return_rows(partial_value, offset):
    summed = lax.psum(partial_value.astype(jnp.bfloat16), "tensor").astype(jnp.float32)
    ready = (summed + offset).astype(jnp.bfloat16)
    return lax.all_to_all(ready, "expert", split_axis=0, concat_axis=0, tiled=True)


def attend_front(normed_b, qkv_weight, images):
    tok_count = normed_b.shape[0]
    head_count = qkv_weight.shape[1] // (3 * DH)
    projected = jnp.dot(normed_b, qkv_weight, preferred_element_type=jnp.float32).astype(
        jnp.bfloat16
    )
    projected = projected.reshape(images, SEQ, head_count, 3, DH)
    queries = projected[:, :, :, 0]
    keys_b = projected[:, :, :, 1]
    values_b = projected[:, :, :, 2]
    scores = jnp.einsum(
        "bqhd,bkhd->bhqk", queries, keys_b, preferred_element_type=jnp.float32
    ) * DH ** (-0.5)
    row_top = jnp.max(scores, axis=3, keepdims=True)
    log_total = row_top + jnp.log(jnp.sum(jnp.exp(scores - row_top), axis=3, keepdims=True))
    attn_b = jnp.exp(scores - log_total).astype(jnp.bfloat16)
    context = jnp.einsum("bhqk,bkhd->bqhd", attn_b, values_b, preferred_element_type=jnp.float32)
    context_b = context.astype(jnp.bfloat16).reshape(tok_count, head_count * DH)
    return (queries, keys_b, values_b, log_total, context_b)


def attend_back(queries, keys_b, values_b, log_total, context_b, context_grad, images):
    tok_count = context_b.shape[0]
    head_count = queries.shape[2]
    factor = DH ** (-0.5)
    scores = (
        jnp.einsum("bqhd,bkhd->bhqk", queries, keys_b, preferred_element_type=jnp.float32) * factor
    )
    attention = jnp.exp(scores - log_total)
    attn_b = attention.astype(jnp.bfloat16)
    grad_ctx = context_grad.reshape(images, SEQ, head_count, DH)
    context_four = context_b.reshape(images, SEQ, head_count, DH)
    value_grad = jnp.einsum("bhqk,bqhd->bkhd", attn_b, grad_ctx, preferred_element_type=jnp.float32)
    attn_grad = jnp.einsum(
        "bqhd,bkhd->bhqk", grad_ctx, values_b, preferred_element_type=jnp.float32
    )
    row_dot = jnp.sum(grad_ctx.astype(jnp.float32) * context_four.astype(jnp.float32), axis=3)
    row_dot = jnp.transpose(row_dot, (0, 2, 1))[:, :, :, None]
    score_grad = (attention * (attn_grad - row_dot) * factor).astype(jnp.bfloat16)
    query_grad = jnp.einsum(
        "bhqk,bkhd->bqhd", score_grad, keys_b, preferred_element_type=jnp.float32
    )
    key_grad = jnp.einsum(
        "bhqk,bqhd->bkhd", score_grad, queries, preferred_element_type=jnp.float32
    )
    stacked = jnp.stack([query_grad, key_grad, value_grad], axis=3)
    return stacked.astype(jnp.bfloat16).reshape(tok_count, head_count * 3 * DH)


def plain_device(
    tokens,
    norm1_gain,
    norm1_shift,
    qkv_weight,
    proj_weight,
    proj_shift,
    norm2_gain,
    norm2_shift,
    router_weight,
    expand_weight,
    expand_shift,
    shrink_weight,
    shrink_shift,
    route_expert,
    route_slot,
    cotangent,
):
    experts = lax.axis_size("expert")
    tensor_count = lax.axis_size("tensor")
    tok_count = tokens.shape[0]
    images = tok_count // SEQ
    capacity = tensor_count * (5 * tok_count // (2 * experts * tensor_count) + 1)
    width = tokens.shape[1]
    token_f = tokens.astype(jnp.float32)
    normed, scaled1, inverse1 = normalize(token_f, norm1_gain, norm1_shift)
    normed_b = normed.astype(jnp.bfloat16)
    queries, keys_b, values_b, log_total, context_b = attend_front(normed_b, qkv_weight, images)
    attn_part = jnp.dot(context_b, proj_weight, preferred_element_type=jnp.float32)
    hidden = token_f + heads_total(attn_part) + proj_shift
    normed2, scaled2, inverse2 = normalize(hidden, norm2_gain, norm2_shift)
    mixed_b = normed2.astype(jnp.bfloat16)
    logits = jnp.dot(mixed_b, router_weight, preferred_element_type=jnp.float32)
    pick_mask = (
        lax.broadcasted_iota(jnp.int32, (tok_count, 2, experts), 2) == route_expert[:, :, None]
    ).astype(jnp.float32)
    chosen = jnp.sum(logits[:, None, :] * pick_mask, axis=2)
    gate_top = jnp.max(chosen, axis=1, keepdims=True)
    lifted = jnp.exp(chosen - gate_top)
    gate_weights = lifted / jnp.sum(lifted, axis=1, keepdims=True)
    targets, owners = route_tables(route_expert, route_slot, experts, capacity)
    buffer = jnp.take(mixed_b, owners // 2, axis=0, mode="fill", fill_value=0).reshape(
        experts, capacity, width
    )
    received = send_rows(buffer).reshape(experts * capacity, width)
    preact = (
        jnp.dot(received, expand_weight[0], preferred_element_type=jnp.float32) + expand_shift[0]
    )
    activ_b = gelu_exact(preact).astype(jnp.bfloat16)
    out_part = jnp.dot(activ_b, shrink_weight[0], preferred_element_type=jnp.float32).reshape(
        experts, capacity, width
    )
    returned = return_rows(out_part, shrink_shift[0]).reshape(experts * capacity, width)
    picked = (
        jnp.take(returned, targets, axis=0, mode="fill", fill_value=0)
        .reshape(tok_count, 2, width)
        .astype(jnp.float32)
    )
    output = hidden + jnp.sum(gate_weights[:, :, None] * picked, axis=1)
    upstream = cotangent.astype(jnp.float32)
    gate_grad = jnp.sum(upstream[:, None, :] * picked, axis=2)
    weighted = (
        (gate_weights[:, :, None] * upstream[:, None, :])
        .astype(jnp.bfloat16)
        .reshape(2 * tok_count, width)
    )
    grad_buffer = jnp.take(weighted, owners, axis=0, mode="fill", fill_value=0).reshape(
        experts, capacity, width
    )
    grad_recv = send_rows(grad_buffer).reshape(experts * capacity, width)
    shrink_g = inner_rows(activ_b, grad_recv)
    sshift_g = jnp.sum(grad_recv.astype(jnp.float32), axis=0)
    pre_grad = outer_cols(grad_recv, shrink_weight[0]) * gelu_slope(preact)
    pre_gradb = pre_grad.astype(jnp.bfloat16)
    expand_g = inner_rows(received, pre_gradb)
    eshift_g = jnp.sum(pre_grad, axis=0)
    rows_part = outer_cols(pre_gradb, expand_weight[0]).reshape(experts, capacity, width)
    back_rows = return_rows(rows_part, 0.0).reshape(experts * capacity, width)
    common = jnp.sum(gate_weights * gate_grad, axis=1, keepdims=True)
    chosen_grad = gate_weights * (gate_grad - common)
    logit_grad = jnp.sum(pick_mask * chosen_grad[:, :, None], axis=1).astype(jnp.bfloat16)
    router_g = inner_rows(mixed_b, logit_grad)
    back_pick = (
        jnp.take(back_rows, targets, axis=0, mode="fill", fill_value=0)
        .reshape(tok_count, 2, width)
        .astype(jnp.float32)
    )
    mixed_grad = jnp.sum(back_pick, axis=1) + outer_cols(logit_grad, router_weight)
    gain2_g = jnp.sum(mixed_grad * scaled2, axis=0)
    shift2_g = jnp.sum(mixed_grad, axis=0)
    hidden_grad = upstream + norm_back(mixed_grad, scaled2, inverse2, norm2_gain)
    pshift_g = jnp.sum(hidden_grad, axis=0)
    hidden_gradb = hidden_grad.astype(jnp.bfloat16)
    proj_g = inner_rows(context_b, hidden_gradb)
    context_grad = outer_cols(hidden_gradb, proj_weight).astype(jnp.bfloat16)
    qkv_gradb = attend_back(queries, keys_b, values_b, log_total, context_b, context_grad, images)
    qkv_g = inner_rows(normed_b, qkv_gradb)
    normed_grad = heads_total(outer_cols(qkv_gradb, qkv_weight))
    gain1_g = jnp.sum(normed_grad * scaled1, axis=0)
    shift1_g = jnp.sum(normed_grad, axis=0)
    tokens_grad = hidden_grad + norm_back(normed_grad, scaled1, inverse1, norm1_gain)
    summed = lax.psum(
        (gain1_g, shift1_g, qkv_g, proj_g, pshift_g, gain2_g, shift2_g, router_g), "expert"
    )
    return (
        output,
        tokens_grad,
        summed[0],
        summed[1],
        summed[2],
        summed[3],
        summed[4],
        summed[5],
        summed[6],
        summed[7],
        expand_g[None],
        eshift_g[None],
        shrink_g[None],
        sshift_g[None],
    )

MESH = pl.DeviceIdType.MESH
F32 = jnp.float32
BF16 = jnp.bfloat16


def place():
    e = lax.axis_index("expert")
    t = lax.axis_index("tensor")
    a = t // 2
    c = t % 2
    return e, t, a, c, (e, 2 * a + 1 - c), (e, 2 * (1 - a) + c)


def greet(devices):
    barrier = pltpu.get_barrier_semaphore()
    for device in devices:
        pl.semaphore_signal(barrier, inc=1, device_id=device, device_id_type=MESH)
    pl.semaphore_wait(barrier, len(devices))


def remote(src, dst, send, recv, device):
    return pltpu.make_async_remote_copy(
        src_ref=src, dst_ref=dst, send_sem=send, recv_sem=recv, device_id=device, device_id_type=MESH
    )


def turns(count):
    far = list(range(count // 2, count))
    near = list(range(1, count // 2))
    order = []
    for i, step in enumerate(far):
        order.append(step)
        if i < len(near):
            order.append(near[i])
    return order


def lanes(index, width):
    return pl.ds(pl.multiple_of(index * width, 128), width)


def call(kernel, outs, scratch, number, args):
    vmem = pl.BlockSpec(memory_space=pltpu.VMEM)
    return pl.pallas_call(
        kernel,
        out_shape=outs,
        in_specs=[vmem] * len(args),
        out_specs=jax.tree.map(lambda _: vmem, outs),
        scratch_shapes=scratch,
        compiler_params=pltpu.CompilerParams(
            collective_id=number, has_side_effects=True, vmem_limit_bytes=48 * 1024 * 1024
        ),
    )(*args)


def tensor_sum_kernel(x, out, got1, part, got2, send, recv):
    e, t, a, c, core, across = place()
    greet([core, across])
    half = x.shape[1] // 2
    mine, other = lanes(c, half), lanes(1 - c, half)
    copy = remote(x.at[:, other], got1, send.at[0], recv.at[0], core)
    copy.start()
    copy.wait()
    part[...] = (x[:, mine].astype(F32) + got1[...].astype(F32)).astype(BF16)
    copy = remote(part, got2, send.at[1], recv.at[1], across)
    copy.start()
    copy.wait()
    out[:, mine] = (part[...].astype(F32) + got2[...].astype(F32)).astype(BF16)
    copy = remote(out.at[:, mine], out.at[:, mine], send.at[2], recv.at[2], core)
    copy.start()
    copy.wait()


def tensor_sum(x, number):
    rows, width = x.shape
    half = pltpu.VMEM((rows, width // 2), BF16)
    sems = pltpu.SemaphoreType.DMA((3,))
    return call(
        tensor_sum_kernel,
        jax.ShapeDtypeStruct((rows, width), BF16),
        [half, half, half, sems, sems],
        number,
        (x,),
    )


def dispatch_kernel(first, second, out0, out1, send_far, send_across, send_core, recv, local):
    e, t, a, c, core, across = place()
    count = first.shape[0]
    peers = [(e ^ d, t) for d in range(1, count)]
    greet(peers + [core, across])
    ins, outs = (first, second), (out0, out1)
    sent = []

    def push(src, k, origin, quarter, send, device):
        copy = remote(src, outs[k].at[origin, quarter], send, recv.at[k, origin, quarter], device)
        copy.start()
        sent.append(copy)

    def arrive(k, origin, quarter):
        spot = outs[k].at[origin, quarter]
        remote(spot, spot, send_core.at[k, origin, quarter], recv.at[k, origin, quarter], core).wait_recv()

    for d in turns(count):
        dst = e ^ d
        for k in range(2):
            push(ins[k].at[dst], k, e, t, send_far.at[k, d], (dst, t))
    keeps = []
    for k in range(2):
        push(ins[k].at[e], k, e, t, send_across.at[k, e], across)
        push(ins[k].at[e], k, e, t, send_core.at[k, e, t], core)
        keep = pltpu.make_async_copy(ins[k].at[e], outs[k].at[e, t], local.at[k])
        keep.start()
        keeps.append(keep)
    far = 2 * (1 - a) + c
    order = turns(count)
    for i in range(count):
        if i < count - 1:
            origin = e ^ order[i]
            for k in range(2):
                arrive(k, origin, t)
                push(outs[k].at[origin, t], k, origin, t, send_across.at[k, origin], across)
                push(outs[k].at[origin, t], k, origin, t, send_core.at[k, origin, t], core)
        origin = e ^ order[i - 1] if i else e
        for k in range(2):
            arrive(k, origin, far)
            push(outs[k].at[origin, far], k, origin, far, send_core.at[k, origin, far], core)
    for d in range(count):
        origin = e ^ d
        for k in range(2):
            arrive(k, origin, 2 * a + 1 - c)
            arrive(k, origin, 2 * (1 - a) + 1 - c)
    for copy in sent:
        copy.wait_send()
    for keep in keeps:
        keep.wait()


def dispatch(first, second, number):
    count, rows, width = first.shape
    out = jax.ShapeDtypeStruct((count, 4, rows, width), BF16)
    dma = pltpu.SemaphoreType.DMA
    return call(
        dispatch_kernel,
        (out, out),
        [dma((2, count)), dma((2, count)), dma((2, count, 4)), dma((2, count, 4)), dma((2,))],
        number,
        (first, second),
    )


def collect_kernel(
    part0, part1, shift, out0, out1, got1, half1, got2, ready,
    send1, recv1, send2, recv2, send3, recv3, send4, recv4, local,
):
    e, t, a, c, core, across = place()
    count = part0.shape[0]
    peers = [(e ^ d, t) for d in range(1, count)]
    greet(peers + [core, across])
    parts, outs = (part0, part1), (out0, out1)
    rows = part0.shape[1] // 2
    width = part0.shape[2] // 2
    mine, other = pl.ds(c * rows, rows), pl.ds((1 - c) * rows, rows)
    left, right = lanes(a, width), lanes(1 - a, width)
    order = [e ^ d for d in turns(count)] + [e]
    steps = [(dst, k) for dst in order for k in range(2)]
    stage1, stage2, rest = [], [], []
    for dst, k in steps:
        copy = remote(parts[k].at[dst, other], got1.at[k, dst], send1.at[k, dst], recv1.at[k, dst], core)
        copy.start()
        stage1.append(copy)
    for i, (dst, k) in enumerate(steps):
        stage1[i].wait_recv()
        half1[k, dst] = (parts[k][dst, mine].astype(F32) + got1[k, dst].astype(F32)).astype(BF16)
        copy = remote(
            half1.at[k, dst, :, right], got2.at[k, dst], send2.at[k, dst], recv2.at[k, dst], across
        )
        copy.start()
        stage2.append(copy)
    keeps = []
    for i, (dst, k) in enumerate(steps):
        stage2[i].wait_recv()
        total = half1[k, dst, :, left].astype(F32) + got2[k, dst].astype(F32)
        if k == 0:
            total = total + shift[:, left]
        ready[k, dst] = total.astype(BF16)
        if i < len(steps) - 2:
            copy = remote(ready.at[k, dst], outs[k].at[e, c], send3.at[k, dst], recv3.at[k, e], (dst, t))
            copy.start()
            rest.append(copy)
        else:
            copy = remote(ready.at[k, dst], outs[k].at[e, c], send4.at[k, e], recv4.at[k, e], core)
            copy.start()
            rest.append(copy)
            keep = pltpu.make_async_copy(ready.at[k, dst], outs[k].at[e, c], local.at[k])
            keep.start()
            keeps.append(keep)
    for d in turns(count):
        origin = e ^ d
        for k in range(2):
            spot = outs[k].at[origin, c]
            remote(spot, spot, send4.at[k, origin], recv3.at[k, origin], core).wait_recv()
            copy = remote(spot, spot, send4.at[k, origin], recv4.at[k, origin], core)
            copy.start()
            rest.append(copy)
    for d in range(count):
        origin = e ^ d
        for k in range(2):
            spot = outs[k].at[origin, 1 - c]
            remote(spot, spot, send4.at[k, origin], recv4.at[k, origin], core).wait_recv()
    for copy in stage1 + stage2 + rest:
        copy.wait_send()
    for keep in keeps:
        keep.wait()


def collect(part0, part1, shift, number):
    count, rows, width = part0.shape
    out = jax.ShapeDtypeStruct((count, 2, rows // 2, width // 2), BF16)
    dma = pltpu.SemaphoreType.DMA
    full = pltpu.VMEM((2, count, rows // 2, width), BF16)
    half = pltpu.VMEM((2, count, rows // 2, width // 2), BF16)
    return call(
        collect_kernel,
        (out, out),
        [full, full, half, half] + [dma((2, count))] * 8 + [dma((2,))],
        number,
        (part0, part1, shift),
    )


def swap_kernel(first, second, gate, out0, out1, gate_out, got, send, recv, send_gate, recv_gate):
    e, t, a, c, core, across = place()
    greet([core, across])
    width = first.shape[1]
    mine, other = lanes(a, width), lanes(1 - a, width)
    small = remote(gate, got, send_gate, recv_gate, across)
    small.start()

    def trade(src, out, out_other):
        out_here = out.at[:, mine]
        copy = remote(src, out_here, send.at[0], recv.at[0], across)
        copy.start()
        out0[:, mine] = first[...]
        out1[:, mine] = second[...]
        copy.wait()
        spot = out.at[:, other]
        copy = remote(spot, spot, send.at[1], recv.at[1], core)
        copy.start()
        spot_other = out_other.at[:, other]
        remote(spot_other, spot_other, send.at[1], recv.at[1], core).wait_recv()
        copy.wait_send()

    @pl.when(c == 0)
    def _():
        trade(first, out0, out1)

    @pl.when(c == 1)
    def _():
        trade(second, out1, out0)

    small.wait()
    gate_out[...] = gate[...] + got[...]


def swap(first, second, gate, number):
    rows, width = first.shape
    out = jax.ShapeDtypeStruct((rows, 2 * width), BF16)
    dma = pltpu.SemaphoreType.DMA
    return call(
        swap_kernel,
        (out, out, jax.ShapeDtypeStruct(gate.shape, F32)),
        [pltpu.VMEM(gate.shape, F32), dma((2,)), dma((2,)), dma(()), dma(())],
        number,
        (first, second, gate),
    )


def final_kernel(
    big, small, x, out, out_small, out_x, got1, sgot1, half1, shalf1, got2, sgot2,
    xgot1, xpart, xgot2, tiny, tgot,
    send1, recv1, send2, recv2, send3, recv3, send4, recv4, xsend, xrecv, tsend, trecv,
):
    e, t, a, c, core, across = place()
    z = e // 2
    y = e % 2
    deep = big.shape[0] // 2
    beside = (2 * z + 1 - y, t)
    greet([beside, core, across] + [(2 * lax.rem(z + d, deep) + y, t) for d in range(1, deep)])
    width = x.shape[1] // 2
    mine, other = lanes(c, width), lanes(1 - c, width)
    xcopies = [
        remote(x.at[:, other], xgot1, xsend.at[0], xrecv.at[0], core),
        remote(xpart, xgot2, xsend.at[1], xrecv.at[1], across),
        remote(out_x.at[:, mine], out_x.at[:, mine], xsend.at[2], xrecv.at[2], core),
    ]
    xcopies[0].start()
    stage1, stage2, rest = [], [], []
    order = [2, 1, 3, 0]
    for d in order:
        zz = lax.rem(z + d, deep)
        chunk = 2 * zz + 1 - y
        pair = (
            remote(big.at[chunk], got1.at[zz], send1.at[0, zz], recv1.at[0, zz], beside),
            remote(small.at[chunk], sgot1.at[zz], send1.at[1, zz], recv1.at[1, zz], beside),
        )
        for copy in pair:
            copy.start()
        stage1.append(pair)
    xcopies[0].wait()
    xpart[...] = (x[:, mine].astype(F32) + xgot1[...].astype(F32)).astype(BF16)
    xcopies[1].start()
    for i, d in enumerate(order):
        zz = lax.rem(z + d, deep)
        chunk = 2 * zz + y
        for copy in stage1[i]:
            copy.wait_recv()
        half1[zz] = (big[chunk].astype(F32) + got1[zz].astype(F32)).astype(BF16)
        shalf1[zz] = small[chunk] + sgot1[zz]
        if d:
            for copy in (
                remote(half1.at[zz], got2.at[z], send2.at[0, zz], recv2.at[0, z], (chunk, t)),
                remote(shalf1.at[zz], sgot2.at[z], send2.at[1, zz], recv2.at[1, z], (chunk, t)),
            ):
                copy.start()
                rest.append(copy)
    total = half1[z].astype(F32)
    stotal = shalf1[z]
    for d in (3, 1, 2):
        zz = lax.rem(z + d, deep)
        spot, sspot = got2.at[zz], sgot2.at[zz]
        remote(spot, spot, send2.at[0, zz], recv2.at[0, zz], beside).wait_recv()
        remote(sspot, sspot, send2.at[1, zz], recv2.at[1, zz], beside).wait_recv()
        total = total + got2[zz].astype(F32)
        stotal = stotal + sgot2[zz]
    out[e] = total.astype(BF16)
    both = (out, out_small)

    def spread(k):
        spot = both[k].at[e]
        for d in (2, 1, 3):
            zz = lax.rem(z + d, deep)
            copy = remote(spot, spot, send3.at[k, zz], recv3.at[k, z], (2 * zz + y, t))
            copy.start()
            rest.append(copy)

    spread(0)
    tiny[0] = stotal
    copy = remote(tiny.at[0], tgot.at[0], tsend.at[0], trecv.at[0], core)
    copy.start()
    copy.wait()
    tiny[1] = stotal + tgot[0]
    copy = remote(tiny.at[1], tgot.at[1], tsend.at[1], trecv.at[1], across)
    copy.start()
    copy.wait()
    out_small[e] = tiny[1] + tgot[1]
    spread(1)
    xcopies[1].wait()
    out_x[:, mine] = (xpart[...].astype(F32) + xgot2[...].astype(F32)).astype(BF16)
    xcopies[2].start()
    for d in (0, 3, 1, 2):
        zz = lax.rem(z + d, deep)
        for k in range(2):
            spot = both[k].at[2 * zz + y]
            if d:
                remote(spot, spot, send4.at[k, zz], recv3.at[k, zz], beside).wait_recv()
            copy = remote(spot, spot, send4.at[k, zz], recv4.at[k, zz], beside)
            copy.start()
            rest.append(copy)
    for zz in range(deep):
        for k in range(2):
            spot = both[k].at[2 * zz + 1 - y]
            remote(spot, spot, send4.at[k, zz], recv4.at[k, zz], beside).wait_recv()
    xcopies[2].wait()
    for pair in stage1:
        for copy in pair:
            copy.wait_send()
    for copy in rest:
        copy.wait_send()


def final_sums(big, small, x, number):
    count, rows, width = big.shape
    deep = count // 2
    dma = pltpu.SemaphoreType.DMA
    large = pltpu.VMEM((deep, rows, width), BF16)
    little = pltpu.VMEM((deep,) + small.shape[1:], F32)
    half = pltpu.VMEM((x.shape[0], x.shape[1] // 2), BF16)
    tiny = pltpu.VMEM((2,) + small.shape[1:], F32)
    shapes = [jax.ShapeDtypeStruct(v.shape, v.dtype) for v in (big, small, x)]
    return call(
        final_kernel,
        tuple(shapes),
        [large, little, large, little, large, little, half, half, half, tiny, tiny]
        + [dma((2, deep))] * 8
        + [dma((3,)), dma((3,)), dma((2,)), dma((2,))],
        number,
        (big, small, x),
    )


def fast_device(
    tokens,
    norm1_gain,
    norm1_shift,
    qkv_weight,
    proj_weight,
    proj_shift,
    norm2_gain,
    norm2_shift,
    router_weight,
    expand_weight,
    expand_shift,
    shrink_weight,
    shrink_shift,
    route_expert,
    route_slot,
    cotangent,
):
    experts = lax.axis_size("expert")
    tensor_count = lax.axis_size("tensor")
    tensor_index = lax.axis_index("tensor")
    tok_count = tokens.shape[0]
    images = tok_count // SEQ
    capacity = tensor_count * (5 * tok_count // (2 * experts * tensor_count) + 1)
    quarter = -(-capacity // (16 * tensor_count)) * 16
    padded = quarter * tensor_count
    width = tokens.shape[1]
    half = width // 2
    token_f = tokens.astype(F32)
    normed, scaled1, inverse1 = normalize(token_f, norm1_gain, norm1_shift)
    normed_b = normed.astype(BF16)
    queries, keys_b, values_b, log_total, context_b = attend_front(normed_b, qkv_weight, images)
    attn_part = jnp.dot(context_b, proj_weight, preferred_element_type=F32).astype(BF16)
    hidden = token_f + tensor_sum(attn_part, 1).astype(F32) + proj_shift
    normed2, scaled2, inverse2 = normalize(hidden, norm2_gain, norm2_shift)
    mixed_b = normed2.astype(BF16)
    logits = jnp.dot(mixed_b, router_weight, preferred_element_type=F32)
    picks = [
        lax.broadcasted_iota(jnp.int32, (tok_count, experts), 1) == route_expert[:, j : j + 1]
        for j in range(2)
    ]
    chosen = [jnp.sum(jnp.where(pick, logits, 0.0), axis=1, keepdims=True) for pick in picks]
    gate_top = jnp.maximum(chosen[0], chosen[1])
    lifted = [jnp.exp(value - gate_top) for value in chosen]
    gates = [value / (lifted[0] + lifted[1]) for value in lifted]
    spots = jnp.where(route_slot >= 0, route_expert * padded + route_slot, -1)
    spots_t = spots.T
    row_ids = lax.broadcasted_iota(jnp.int32, (experts, quarter, 1), 0) * padded
    row_ids = row_ids + lax.broadcasted_iota(jnp.int32, (experts, quarter, 1), 1)
    row_ids = (row_ids + tensor_index * quarter).reshape(experts * quarter, 1)
    hits = [row_ids == spots_t[j][None, :] for j in range(2)]
    chooser = (hits[0] | hits[1]).astype(BF16)
    slot_gate = jnp.sum(
        jnp.where(hits[0], gates[0].reshape(1, -1), 0.0)
        + jnp.where(hits[1], gates[1].reshape(1, -1), 0.0),
        axis=1,
        keepdims=True,
    )
    rows_out = jnp.dot(chooser, mixed_b, preferred_element_type=F32).astype(BF16)
    grad_out = (slot_gate * jnp.dot(chooser, cotangent, preferred_element_type=F32)).astype(BF16)
    received, grad_recv = dispatch(
        rows_out.reshape(experts, quarter, width), grad_out.reshape(experts, quarter, width), 2
    )
    received = received.reshape(experts * padded, width)
    grad_recv = grad_recv.reshape(experts * padded, width)
    preact = jnp.dot(received, expand_weight[0], preferred_element_type=F32) + expand_shift[0]
    activ_b = gelu_exact(preact).astype(BF16)
    out_part = jnp.dot(activ_b, shrink_weight[0], preferred_element_type=F32).astype(BF16)
    pre_grad = outer_cols(grad_recv, shrink_weight[0]) * gelu_slope(preact)
    pre_gradb = pre_grad.astype(BF16)
    rows_part = outer_cols(pre_gradb, expand_weight[0]).astype(BF16)
    returned, back_rows = collect(
        out_part.reshape(experts, padded, width),
        rows_part.reshape(experts, padded, width),
        shrink_shift,
        3,
    )
    returned = returned.reshape(experts * padded, half)
    back_rows = back_rows.reshape(experts * padded, half)
    shrink_g = inner_rows(activ_b, grad_recv)
    sshift_g = jnp.sum(grad_recv.astype(F32), axis=0)
    expand_g = inner_rows(received, pre_gradb)
    eshift_g = jnp.sum(pre_grad, axis=0)
    upstream = cotangent.astype(F32)
    slots = lax.broadcasted_iota(jnp.int32, (tok_count, experts * padded), 1)
    marks = [slots == spots[:, j : j + 1] for j in range(2)]
    mixer = (jnp.where(marks[0], gates[0], 0.0) + jnp.where(marks[1], gates[1], 0.0)).astype(BF16)
    gather = (marks[0] | marks[1]).astype(BF16)
    added = jnp.dot(mixer, returned, preferred_element_type=F32).astype(BF16)
    back = jnp.dot(gather, back_rows, preferred_element_type=F32).astype(BF16)
    cot_half = lax.dynamic_slice(cotangent, (0, (tensor_index // 2) * half), (tok_count, half))
    dots = outer_cols(cot_half, returned)
    gate_part = jnp.stack([jnp.sum(jnp.where(mark, dots, 0.0), axis=1) for mark in marks])
    gate_part = jnp.pad(gate_part, ((0, 6), (0, -tok_count % 128)))
    added, back, gate_full = swap(added, back, gate_part, 4)
    output = hidden + added.astype(F32)
    gate_grad = [gate_full[j, :tok_count].reshape(tok_count, 1) for j in range(2)]
    common = gates[0] * gate_grad[0] + gates[1] * gate_grad[1]
    logit_grad = (
        jnp.where(picks[0], gates[0] * (gate_grad[0] - common), 0.0)
        + jnp.where(picks[1], gates[1] * (gate_grad[1] - common), 0.0)
    ).astype(BF16)
    router_g = inner_rows(logit_grad, mixed_b)
    mixed_grad = back.astype(F32) + outer_cols(logit_grad, router_weight)
    gain2_g = jnp.sum(mixed_grad * scaled2, axis=0)
    shift2_g = jnp.sum(mixed_grad, axis=0)
    hidden_grad = upstream + norm_back(mixed_grad, scaled2, inverse2, norm2_gain)
    pshift_g = jnp.sum(hidden_grad, axis=0)
    hidden_gradb = hidden_grad.astype(BF16)
    context_grad = outer_cols(hidden_gradb, proj_weight).astype(BF16)
    qkv_gradb = attend_back(queries, keys_b, values_b, log_total, context_b, context_grad, images)
    normed_part = outer_cols(qkv_gradb, qkv_weight)
    gain1_g = jnp.sum(normed_part * scaled1, axis=0)
    shift1_g = jnp.sum(normed_part, axis=0)
    qkv_g = inner_rows(normed_b, qkv_gradb)
    proj_g = inner_rows(hidden_gradb, context_b)
    big = jnp.concatenate([qkv_g.astype(BF16), proj_g.astype(BF16)], axis=1)
    wide = big.shape[1]
    small = jnp.concatenate(
        [
            jnp.stack([gain1_g, shift1_g]),
            jnp.stack([pshift_g, gain2_g, shift2_g]) / tensor_count,
            router_g / tensor_count,
        ],
        axis=0,
    )
    names = small.shape[0]
    piece = width // experts
    small = jnp.pad(small, ((0, -names % 8), (0, 0)))
    small = small.reshape(small.shape[0], experts, piece).transpose(1, 0, 2)
    small = jnp.pad(small, ((0, 0), (0, 0), (0, -piece % 128)))
    big, small, normed_sum = final_sums(
        big.reshape(experts, piece, wide), small, normed_part.astype(BF16), 6
    )
    normed_grad = normed_sum.astype(F32)
    tokens_grad = hidden_grad + norm_back(normed_grad, scaled1, inverse1, norm1_gain)
    big = big.reshape(width, wide)
    small = small[:, :, :piece].transpose(1, 0, 2).reshape(-1, width)
    return (
        output,
        tokens_grad,
        small[0],
        small[1],
        big[:, : qkv_g.shape[1]].astype(F32),
        big[:, qkv_g.shape[1] :].T.astype(F32),
        small[2],
        small[3],
        small[4],
        small[5:names].T,
        expand_g[None],
        eshift_g[None],
        shrink_g[None],
        sshift_g[None],
    )


def solution(mesh):
    small_mesh = mesh.shape["expert"] == 8 and mesh.shape["tensor"] == 4
    on_device = fast_device if small_mesh else plain_device
    return jax.shard_map(
        on_device,
        mesh=mesh,
        in_specs=(
            P("expert", None),
            P(),
            P(),
            P(None, "tensor"),
            P("tensor", None),
            P(),
            P(),
            P(),
            P(),
            P("expert", None, "tensor"),
            P("expert", "tensor"),
            P("expert", "tensor", None),
            P("expert", None),
            P("expert", None),
            P("expert", None),
            P("expert", None),
        ),
        out_specs=(
            P("expert", None),
            P("expert", None),
            P(),
            P(),
            P(None, "tensor"),
            P("tensor", None),
            P(),
            P(),
            P(),
            P(),
            P("expert", None, "tensor"),
            P("expert", "tensor"),
            P("expert", "tensor", None),
            P("expert", None),
        ),
        check_vma=False,
    )
```

```python
import jax
import jax.numpy as jnp
from jax import lax
from jax.experimental import pallas as pl
from jax.experimental.pallas import tpu as pltpu
from jax.sharding import PartitionSpec as P

DH = 64
SEQ = 197


norm_eps = 1e-06
half_root = 0.7071067811865476
gauss_peak = 0.3989422804014327


def normalize(values, norm_gain, norm_shift):
    row_mean = jnp.mean(values, axis=1, keepdims=True)
    centered = values - row_mean
    variance = jnp.mean(centered * centered, axis=1, keepdims=True)
    inverse = lax.rsqrt(variance + norm_eps)
    scaled = centered * inverse
    return (scaled * norm_gain + norm_shift, scaled, inverse)


def norm_back(upstream, scaled, inverse, norm_gain):
    weighted = upstream * norm_gain
    first_mean = jnp.mean(weighted, axis=1, keepdims=True)
    second_mean = jnp.mean(weighted * scaled, axis=1, keepdims=True)
    return inverse * (weighted - first_mean - scaled * second_mean)


def gelu_exact(preact):
    return 0.5 * preact * (1.0 + lax.erf(preact * half_root))


def gelu_slope(preact):
    return (
        0.5 * (1.0 + lax.erf(preact * half_root))
        + preact * jnp.exp(-0.5 * preact * preact) * gauss_peak
    )


def inner_rows(left_b, right_b):
    return lax.dot_general(
        left_b, right_b, (((0,), (0,)), ((), ())), preferred_element_type=jnp.float32
    )


def outer_cols(left_b, right_b):
    return lax.dot_general(
        left_b, right_b, (((1,), (1,)), ((), ())), preferred_element_type=jnp.float32
    )


def route_tables(route_expert, route_slot, experts, capacity):
    tok_count = route_expert.shape[0]
    kept = route_slot >= 0
    targets = jnp.where(kept, route_expert * capacity + route_slot, experts * capacity).reshape(-1)
    numbers = jnp.arange(2 * tok_count, dtype=jnp.int32)
    owners = (
        jnp.full((experts * capacity,), 2 * tok_count, jnp.int32)
        .at[targets]
        .set(numbers, mode="drop")
    )
    return (targets, owners)


def heads_total(partial_value):
    return lax.psum(partial_value.astype(jnp.bfloat16), "tensor").astype(jnp.float32)


def send_rows(buffer):
    return lax.all_to_all(buffer, "expert", split_axis=0, concat_axis=0, tiled=True)


def return_rows(partial_value, offset):
    summed = lax.psum(partial_value.astype(jnp.bfloat16), "tensor").astype(jnp.float32)
    ready = (summed + offset).astype(jnp.bfloat16)
    return lax.all_to_all(ready, "expert", split_axis=0, concat_axis=0, tiled=True)


def attend_front(normed_b, qkv_weight, images):
    tok_count = normed_b.shape[0]
    head_count = qkv_weight.shape[1] // (3 * DH)
    projected = jnp.dot(normed_b, qkv_weight, preferred_element_type=jnp.float32).astype(
        jnp.bfloat16
    )
    projected = projected.reshape(images, SEQ, head_count, 3, DH)
    queries = projected[:, :, :, 0]
    keys_b = projected[:, :, :, 1]
    values_b = projected[:, :, :, 2]
    scores = jnp.einsum(
        "bqhd,bkhd->bhqk", queries, keys_b, preferred_element_type=jnp.float32
    ) * DH ** (-0.5)
    row_top = jnp.max(scores, axis=3, keepdims=True)
    log_total = row_top + jnp.log(jnp.sum(jnp.exp(scores - row_top), axis=3, keepdims=True))
    attn_b = jnp.exp(scores - log_total).astype(jnp.bfloat16)
    context = jnp.einsum("bhqk,bkhd->bqhd", attn_b, values_b, preferred_element_type=jnp.float32)
    context_b = context.astype(jnp.bfloat16).reshape(tok_count, head_count * DH)
    return (queries, keys_b, values_b, log_total, context_b)


def attend_back(queries, keys_b, values_b, log_total, context_b, context_grad, images):
    tok_count = context_b.shape[0]
    head_count = queries.shape[2]
    factor = DH ** (-0.5)
    scores = (
        jnp.einsum("bqhd,bkhd->bhqk", queries, keys_b, preferred_element_type=jnp.float32) * factor
    )
    attention = jnp.exp(scores - log_total)
    attn_b = attention.astype(jnp.bfloat16)
    grad_ctx = context_grad.reshape(images, SEQ, head_count, DH)
    context_four = context_b.reshape(images, SEQ, head_count, DH)
    value_grad = jnp.einsum("bhqk,bqhd->bkhd", attn_b, grad_ctx, preferred_element_type=jnp.float32)
    attn_grad = jnp.einsum(
        "bqhd,bkhd->bhqk", grad_ctx, values_b, preferred_element_type=jnp.float32
    )
    row_dot = jnp.sum(grad_ctx.astype(jnp.float32) * context_four.astype(jnp.float32), axis=3)
    row_dot = jnp.transpose(row_dot, (0, 2, 1))[:, :, :, None]
    score_grad = (attention * (attn_grad - row_dot) * factor).astype(jnp.bfloat16)
    query_grad = jnp.einsum(
        "bhqk,bkhd->bqhd", score_grad, keys_b, preferred_element_type=jnp.float32
    )
    key_grad = jnp.einsum(
        "bhqk,bqhd->bkhd", score_grad, queries, preferred_element_type=jnp.float32
    )
    stacked = jnp.stack([query_grad, key_grad, value_grad], axis=3)
    return stacked.astype(jnp.bfloat16).reshape(tok_count, head_count * 3 * DH)


def plain_device(
    tokens,
    norm1_gain,
    norm1_shift,
    qkv_weight,
    proj_weight,
    proj_shift,
    norm2_gain,
    norm2_shift,
    router_weight,
    expand_weight,
    expand_shift,
    shrink_weight,
    shrink_shift,
    route_expert,
    route_slot,
    cotangent,
):
    experts = lax.axis_size("expert")
    tensor_count = lax.axis_size("tensor")
    tok_count = tokens.shape[0]
    images = tok_count // SEQ
    capacity = tensor_count * (5 * tok_count // (2 * experts * tensor_count) + 1)
    width = tokens.shape[1]
    token_f = tokens.astype(jnp.float32)
    normed, scaled1, inverse1 = normalize(token_f, norm1_gain, norm1_shift)
    normed_b = normed.astype(jnp.bfloat16)
    queries, keys_b, values_b, log_total, context_b = attend_front(normed_b, qkv_weight, images)
    attn_part = jnp.dot(context_b, proj_weight, preferred_element_type=jnp.float32)
    hidden = token_f + heads_total(attn_part) + proj_shift
    normed2, scaled2, inverse2 = normalize(hidden, norm2_gain, norm2_shift)
    mixed_b = normed2.astype(jnp.bfloat16)
    logits = jnp.dot(mixed_b, router_weight, preferred_element_type=jnp.float32)
    pick_mask = (
        lax.broadcasted_iota(jnp.int32, (tok_count, 2, experts), 2) == route_expert[:, :, None]
    ).astype(jnp.float32)
    chosen = jnp.sum(logits[:, None, :] * pick_mask, axis=2)
    gate_top = jnp.max(chosen, axis=1, keepdims=True)
    lifted = jnp.exp(chosen - gate_top)
    gate_weights = lifted / jnp.sum(lifted, axis=1, keepdims=True)
    targets, owners = route_tables(route_expert, route_slot, experts, capacity)
    buffer = jnp.take(mixed_b, owners // 2, axis=0, mode="fill", fill_value=0).reshape(
        experts, capacity, width
    )
    received = send_rows(buffer).reshape(experts * capacity, width)
    preact = (
        jnp.dot(received, expand_weight[0], preferred_element_type=jnp.float32) + expand_shift[0]
    )
    activ_b = gelu_exact(preact).astype(jnp.bfloat16)
    out_part = jnp.dot(activ_b, shrink_weight[0], preferred_element_type=jnp.float32).reshape(
        experts, capacity, width
    )
    returned = return_rows(out_part, shrink_shift[0]).reshape(experts * capacity, width)
    picked = (
        jnp.take(returned, targets, axis=0, mode="fill", fill_value=0)
        .reshape(tok_count, 2, width)
        .astype(jnp.float32)
    )
    output = hidden + jnp.sum(gate_weights[:, :, None] * picked, axis=1)
    upstream = cotangent.astype(jnp.float32)
    gate_grad = jnp.sum(upstream[:, None, :] * picked, axis=2)
    weighted = (
        (gate_weights[:, :, None] * upstream[:, None, :])
        .astype(jnp.bfloat16)
        .reshape(2 * tok_count, width)
    )
    grad_buffer = jnp.take(weighted, owners, axis=0, mode="fill", fill_value=0).reshape(
        experts, capacity, width
    )
    grad_recv = send_rows(grad_buffer).reshape(experts * capacity, width)
    shrink_g = inner_rows(activ_b, grad_recv)
    sshift_g = jnp.sum(grad_recv.astype(jnp.float32), axis=0)
    pre_grad = outer_cols(grad_recv, shrink_weight[0]) * gelu_slope(preact)
    pre_gradb = pre_grad.astype(jnp.bfloat16)
    expand_g = inner_rows(received, pre_gradb)
    eshift_g = jnp.sum(pre_grad, axis=0)
    rows_part = outer_cols(pre_gradb, expand_weight[0]).reshape(experts, capacity, width)
    back_rows = return_rows(rows_part, 0.0).reshape(experts * capacity, width)
    common = jnp.sum(gate_weights * gate_grad, axis=1, keepdims=True)
    chosen_grad = gate_weights * (gate_grad - common)
    logit_grad = jnp.sum(pick_mask * chosen_grad[:, :, None], axis=1).astype(jnp.bfloat16)
    router_g = inner_rows(mixed_b, logit_grad)
    back_pick = (
        jnp.take(back_rows, targets, axis=0, mode="fill", fill_value=0)
        .reshape(tok_count, 2, width)
        .astype(jnp.float32)
    )
    mixed_grad = jnp.sum(back_pick, axis=1) + outer_cols(logit_grad, router_weight)
    gain2_g = jnp.sum(mixed_grad * scaled2, axis=0)
    shift2_g = jnp.sum(mixed_grad, axis=0)
    hidden_grad = upstream + norm_back(mixed_grad, scaled2, inverse2, norm2_gain)
    pshift_g = jnp.sum(hidden_grad, axis=0)
    hidden_gradb = hidden_grad.astype(jnp.bfloat16)
    proj_g = inner_rows(context_b, hidden_gradb)
    context_grad = outer_cols(hidden_gradb, proj_weight).astype(jnp.bfloat16)
    qkv_gradb = attend_back(queries, keys_b, values_b, log_total, context_b, context_grad, images)
    qkv_g = inner_rows(normed_b, qkv_gradb)
    normed_grad = heads_total(outer_cols(qkv_gradb, qkv_weight))
    gain1_g = jnp.sum(normed_grad * scaled1, axis=0)
    shift1_g = jnp.sum(normed_grad, axis=0)
    tokens_grad = hidden_grad + norm_back(normed_grad, scaled1, inverse1, norm1_gain)
    summed = lax.psum(
        (gain1_g, shift1_g, qkv_g, proj_g, pshift_g, gain2_g, shift2_g, router_g), "expert"
    )
    return (
        output,
        tokens_grad,
        summed[0],
        summed[1],
        summed[2],
        summed[3],
        summed[4],
        summed[5],
        summed[6],
        summed[7],
        expand_g[None],
        eshift_g[None],
        shrink_g[None],
        sshift_g[None],
    )

MESH = pl.DeviceIdType.MESH
F32 = jnp.float32
BF16 = jnp.bfloat16


def place():
    e = lax.axis_index("expert")
    t = lax.axis_index("tensor")
    a = t // 2
    c = t % 2
    return e, t, a, c, (e, 2 * a + 1 - c), (e, 2 * (1 - a) + c)


def greet(devices):
    barrier = pltpu.get_barrier_semaphore()
    for device in devices:
        pl.semaphore_signal(barrier, inc=1, device_id=device, device_id_type=MESH)
    pl.semaphore_wait(barrier, len(devices))


def remote(src, dst, send, recv, device):
    return pltpu.make_async_remote_copy(
        src_ref=src, dst_ref=dst, send_sem=send, recv_sem=recv, device_id=device, device_id_type=MESH
    )


def turns(count):
    far = list(range(count // 2, count))
    near = list(range(1, count // 2))
    order = []
    for i, step in enumerate(far):
        order.append(step)
        if i < len(near):
            order.append(near[i])
    return order


def lanes(index, width):
    return pl.ds(pl.multiple_of(index * width, 128), width)


def call(kernel, outs, scratch, number, args):
    vmem = pl.BlockSpec(memory_space=pltpu.VMEM)
    return pl.pallas_call(
        kernel,
        out_shape=outs,
        in_specs=[vmem] * len(args),
        out_specs=jax.tree.map(lambda _: vmem, outs),
        scratch_shapes=scratch,
        compiler_params=pltpu.CompilerParams(
            collective_id=number, has_side_effects=True, vmem_limit_bytes=48 * 1024 * 1024
        ),
    )(*args)


def tensor_sum_kernel(x, out, got1, part, got2, send, recv):
    e, t, a, c, core, across = place()
    greet([core, across])
    half = x.shape[1] // 2
    mine, other = lanes(c, half), lanes(1 - c, half)
    copy = remote(x.at[:, other], got1, send.at[0], recv.at[0], core)
    copy.start()
    copy.wait()
    part[...] = (x[:, mine].astype(F32) + got1[...].astype(F32)).astype(BF16)
    copy = remote(part, got2, send.at[1], recv.at[1], across)
    copy.start()
    copy.wait()
    out[:, mine] = (part[...].astype(F32) + got2[...].astype(F32)).astype(BF16)
    copy = remote(out.at[:, mine], out.at[:, mine], send.at[2], recv.at[2], core)
    copy.start()
    copy.wait()


def tensor_sum(x, number):
    rows, width = x.shape
    half = pltpu.VMEM((rows, width // 2), BF16)
    sems = pltpu.SemaphoreType.DMA((3,))
    return call(
        tensor_sum_kernel,
        jax.ShapeDtypeStruct((rows, width), BF16),
        [half, half, half, sems, sems],
        number,
        (x,),
    )


def expert_kernel(
    first, second, up_w, up_b, down_w, shift,
    rows_in, grads_in, activ, pre_b, bias_grad, out0, out1,
    part, got1, half1, got2, ready,
    send_far, send_across, send_core, recv,
    send1, recv1, send2, recv2, send3, recv3, send4, recv4, local,
):
    e, t, a, c, core, across = place()
    count = first.shape[0]
    greet([(e ^ d, t) for d in range(1, count)] + [core, across])
    ins, taken, outs = (first, second), (rows_in, grads_in), (out0, out1)
    far = 2 * (1 - a) + c
    near, cross = 2 * a + 1 - c, 2 * (1 - a) + 1 - c
    rows, width = part.shape[2] // 2, part.shape[3] // 2
    mine, other = pl.ds(c * rows, rows), pl.ds((1 - c) * rows, rows)
    left, right = lanes(a, width), lanes(1 - a, width)

    def origin_of(i):
        return e ^ (i // 2 + (i % 2) * (count // 2))

    def far_copy(k, dst):
        return remote(ins[k].at[dst], taken[k].at[e, t], send_far.at[k, dst], recv.at[k, e, t], (dst, t))

    def across_copy(k, origin):
        spot = taken[k].at[origin, t]
        return remote(spot, spot, send_across.at[k, origin], recv.at[k, origin, t], across)

    def core_copy(k, origin, quarter):
        spot = taken[k].at[origin, quarter]
        return remote(spot, spot, send_core.at[k, origin, quarter], recv.at[k, origin, quarter], core)

    def one_copy(k, dst):
        return remote(part.at[k, dst, other], got1.at[k, dst], send1.at[k, dst], recv1.at[k, dst], core)

    def two_copy(k, dst):
        return remote(
            half1.at[k, dst, :, right], got2.at[k, dst], send2.at[k, dst], recv2.at[k, dst], across
        )

    def three_copy(k, dst):
        return remote(ready.at[k, dst], outs[k].at[e, c], send3.at[k, dst], recv3.at[k, e], (dst, t))

    def four_copy(k, origin, side):
        spot = outs[k].at[origin, side]
        return remote(spot, spot, send4.at[k, origin], recv4.at[k, origin], core)

    for d in turns(count):
        for k in range(2):
            far_copy(k, e ^ d).start()
    keeps = [pltpu.make_async_copy(ins[k].at[e], taken[k].at[e, t], local.at[k]) for k in range(2)]
    for keep in keeps:
        keep.start()
    bias_grad[...] = jnp.zeros_like(bias_grad)
    for keep in keeps:
        keep.wait()

    def step(i, carry):
        @pl.when(i < count)
        def _():
            origin = origin_of(i)
            for k in range(2):

                @pl.when(i > 0)
                def _():
                    core_copy(k, origin, t).wait_recv()

                across_copy(k, origin).start()
                core_copy(k, origin, t).start()

        @pl.when((i >= 1) & (i < count + 1))
        def _():
            origin = origin_of(i - 1)
            for k in range(2):
                core_copy(k, origin, far).wait_recv()
                core_copy(k, origin, far).start()

        @pl.when((i >= 2) & (i < count + 2))
        def _():
            origin = origin_of(i - 2)
            for k in range(2):
                core_copy(k, origin, near).wait_recv()
                core_copy(k, origin, cross).wait_recv()
            tokens = rows_in[origin].reshape(2 * rows, 2 * width)
            grads = grads_in[origin].reshape(2 * rows, 2 * width)
            preact = jnp.dot(tokens, up_w[...], preferred_element_type=F32) + up_b[...]
            bell = 0.5 * (1.0 + lax.erf(preact * half_root))
            active = (preact * bell).astype(BF16)
            activ[origin] = active
            part[0, origin] = jnp.dot(active, down_w[...], preferred_element_type=F32).astype(BF16)
            one_copy(0, origin).start()
            slope = bell + preact * jnp.exp(-0.5 * preact * preact) * gauss_peak
            pre_grad = outer_cols(grads, down_w[...]) * slope
            bias_grad[...] += jnp.sum(pre_grad, axis=0, keepdims=True)
            pre_low = pre_grad.astype(BF16)
            pre_b[origin] = pre_low
            part[1, origin] = outer_cols(pre_low, up_w[...]).astype(BF16)
            one_copy(1, origin).start()

        @pl.when((i >= 3) & (i < count + 3))
        def _():
            dst = origin_of(i - 3)
            for k in range(2):
                one_copy(k, dst).wait_recv()
                half1[k, dst] = (
                    part[k, dst, mine].astype(F32) + got1[k, dst].astype(F32)
                ).astype(BF16)
                two_copy(k, dst).start()

        @pl.when(i >= 4)
        def _():
            dst = origin_of(i - 4)
            for k in range(2):
                two_copy(k, dst).wait_recv()
                total = half1[k, dst, :, left].astype(F32) + got2[k, dst].astype(F32)
                if k == 0:
                    total = total + shift[:, left]
                ready[k, dst] = total.astype(BF16)

                @pl.when(i == 4)
                def _():
                    keep = pltpu.make_async_copy(ready.at[k, dst], outs[k].at[e, c], local.at[k])
                    keep.start()
                    keep.wait()
                    four_copy(k, e, c).start()

                @pl.when(i > 4)
                def _():
                    three_copy(k, dst).start()

        return carry

    lax.fori_loop(0, count + 4, step, 0)
    for d in turns(count):
        origin = e ^ d
        for k in range(2):
            spot = outs[k].at[origin, c]
            remote(spot, spot, send4.at[k, origin], recv3.at[k, origin], core).wait_recv()
            four_copy(k, origin, c).start()

    def finish(d, carry):
        origin = e ^ d
        for k in range(2):
            four_copy(k, origin, 1 - c).wait_recv()
            across_copy(k, origin).wait_send()
            core_copy(k, origin, t).wait_send()
            core_copy(k, origin, far).wait_send()
            one_copy(k, origin).wait_send()
            two_copy(k, origin).wait_send()
            four_copy(k, origin, c).wait_send()

            @pl.when(d > 0)
            def _():
                far_copy(k, origin).wait_send()
                three_copy(k, origin).wait_send()

        return carry

    lax.fori_loop(0, count, finish, 0)


def run_experts(first, second, up_w, up_b, down_w, shift, number):
    count, rows, width = first.shape
    hidden = up_w.shape[1]
    taken = jax.ShapeDtypeStruct((count, 4, rows, width), BF16)
    inner = jax.ShapeDtypeStruct((count, 4 * rows, hidden), BF16)
    out = jax.ShapeDtypeStruct((count, 2, 2 * rows, width // 2), BF16)
    dma = pltpu.SemaphoreType.DMA
    full = pltpu.VMEM((2, count, 2 * rows, width), BF16)
    half = pltpu.VMEM((2, count, 2 * rows, width // 2), BF16)
    return call(
        expert_kernel,
        (taken, taken, inner, inner, jax.ShapeDtypeStruct((1, hidden), F32), out, out),
        [pltpu.VMEM((2, count, 4 * rows, width), BF16), full, full, half, half]
        + [dma((2, count)), dma((2, count)), dma((2, count, 4)), dma((2, count, 4))]
        + [dma((2, count))] * 8
        + [dma((2,))],
        number,
        (first, second, up_w, up_b, down_w, shift),
    )


def swap_kernel(first, second, gate, out0, out1, gate_out, got, send, recv, send_gate, recv_gate):
    e, t, a, c, core, across = place()
    greet([core, across])
    width = first.shape[1]
    mine, other = lanes(a, width), lanes(1 - a, width)
    small = remote(gate, got, send_gate, recv_gate, across)
    small.start()

    def trade(src, out, out_other):
        out_here = out.at[:, mine]
        copy = remote(src, out_here, send.at[0], recv.at[0], across)
        copy.start()
        out0[:, mine] = first[...]
        out1[:, mine] = second[...]
        copy.wait()
        spot = out.at[:, other]
        copy = remote(spot, spot, send.at[1], recv.at[1], core)
        copy.start()
        spot_other = out_other.at[:, other]
        remote(spot_other, spot_other, send.at[1], recv.at[1], core).wait_recv()
        copy.wait_send()

    @pl.when(c == 0)
    def _():
        trade(first, out0, out1)

    @pl.when(c == 1)
    def _():
        trade(second, out1, out0)

    small.wait()
    gate_out[...] = gate[...] + got[...]


def swap(first, second, gate, number):
    rows, width = first.shape
    out = jax.ShapeDtypeStruct((rows, 2 * width), BF16)
    dma = pltpu.SemaphoreType.DMA
    return call(
        swap_kernel,
        (out, out, jax.ShapeDtypeStruct(gate.shape, F32)),
        [pltpu.VMEM(gate.shape, F32), dma((2,)), dma((2,)), dma(()), dma(())],
        number,
        (first, second, gate),
    )


def final_kernel(
    big, small, x, out, out_small, out_x, got1, sgot1, half1, shalf1, got2, sgot2,
    xgot1, xpart, xgot2, tiny, tgot,
    send1, recv1, send2, recv2, send3, recv3, send4, recv4, xsend, xrecv, tsend, trecv,
):
    e, t, a, c, core, across = place()
    z = e // 2
    y = e % 2
    deep = big.shape[0] // 2
    beside = (2 * z + 1 - y, t)
    greet([beside, core, across] + [(2 * lax.rem(z + d, deep) + y, t) for d in range(1, deep)])
    width = x.shape[1] // 2
    mine, other = lanes(c, width), lanes(1 - c, width)
    xcopies = [
        remote(x.at[:, other], xgot1, xsend.at[0], xrecv.at[0], core),
        remote(xpart, xgot2, xsend.at[1], xrecv.at[1], across),
        remote(out_x.at[:, mine], out_x.at[:, mine], xsend.at[2], xrecv.at[2], core),
    ]
    xcopies[0].start()
    stage1, stage2, rest = [], [], []
    order = [2, 1, 3, 0]
    for d in order:
        zz = lax.rem(z + d, deep)
        chunk = 2 * zz + 1 - y
        pair = (
            remote(big.at[chunk], got1.at[zz], send1.at[0, zz], recv1.at[0, zz], beside),
            remote(small.at[chunk], sgot1.at[zz], send1.at[1, zz], recv1.at[1, zz], beside),
        )
        for copy in pair:
            copy.start()
        stage1.append(pair)
    xcopies[0].wait()
    xpart[...] = (x[:, mine].astype(F32) + xgot1[...].astype(F32)).astype(BF16)
    xcopies[1].start()
    for i, d in enumerate(order):
        zz = lax.rem(z + d, deep)
        chunk = 2 * zz + y
        for copy in stage1[i]:
            copy.wait_recv()
        half1[zz] = (big[chunk].astype(F32) + got1[zz].astype(F32)).astype(BF16)
        shalf1[zz] = small[chunk] + sgot1[zz]
        if d:
            for copy in (
                remote(half1.at[zz], got2.at[z], send2.at[0, zz], recv2.at[0, z], (chunk, t)),
                remote(shalf1.at[zz], sgot2.at[z], send2.at[1, zz], recv2.at[1, z], (chunk, t)),
            ):
                copy.start()
                rest.append(copy)
    total = half1[z].astype(F32)
    stotal = shalf1[z]
    for d in (3, 1, 2):
        zz = lax.rem(z + d, deep)
        spot, sspot = got2.at[zz], sgot2.at[zz]
        remote(spot, spot, send2.at[0, zz], recv2.at[0, zz], beside).wait_recv()
        remote(sspot, sspot, send2.at[1, zz], recv2.at[1, zz], beside).wait_recv()
        total = total + got2[zz].astype(F32)
        stotal = stotal + sgot2[zz]
    out[e] = total.astype(BF16)
    both = (out, out_small)

    def spread(k):
        spot = both[k].at[e]
        for d in (2, 1, 3):
            zz = lax.rem(z + d, deep)
            copy = remote(spot, spot, send3.at[k, zz], recv3.at[k, z], (2 * zz + y, t))
            copy.start()
            rest.append(copy)

    spread(0)
    tiny[0] = stotal
    copy = remote(tiny.at[0], tgot.at[0], tsend.at[0], trecv.at[0], core)
    copy.start()
    copy.wait()
    tiny[1] = stotal + tgot[0]
    copy = remote(tiny.at[1], tgot.at[1], tsend.at[1], trecv.at[1], across)
    copy.start()
    copy.wait()
    out_small[e] = tiny[1] + tgot[1]
    spread(1)
    xcopies[1].wait()
    out_x[:, mine] = (xpart[...].astype(F32) + xgot2[...].astype(F32)).astype(BF16)
    xcopies[2].start()
    for d in (0, 3, 1, 2):
        zz = lax.rem(z + d, deep)
        for k in range(2):
            spot = both[k].at[2 * zz + y]
            if d:
                remote(spot, spot, send4.at[k, zz], recv3.at[k, zz], beside).wait_recv()
            copy = remote(spot, spot, send4.at[k, zz], recv4.at[k, zz], beside)
            copy.start()
            rest.append(copy)
    for zz in range(deep):
        for k in range(2):
            spot = both[k].at[2 * zz + 1 - y]
            remote(spot, spot, send4.at[k, zz], recv4.at[k, zz], beside).wait_recv()
    xcopies[2].wait()
    for pair in stage1:
        for copy in pair:
            copy.wait_send()
    for copy in rest:
        copy.wait_send()


def final_sums(big, small, x, number):
    count, rows, width = big.shape
    deep = count // 2
    dma = pltpu.SemaphoreType.DMA
    large = pltpu.VMEM((deep, rows, width), BF16)
    little = pltpu.VMEM((deep,) + small.shape[1:], F32)
    half = pltpu.VMEM((x.shape[0], x.shape[1] // 2), BF16)
    tiny = pltpu.VMEM((2,) + small.shape[1:], F32)
    shapes = [jax.ShapeDtypeStruct(v.shape, v.dtype) for v in (big, small, x)]
    return call(
        final_kernel,
        tuple(shapes),
        [large, little, large, little, large, little, half, half, half, tiny, tiny]
        + [dma((2, deep))] * 8
        + [dma((3,)), dma((3,)), dma((2,)), dma((2,))],
        number,
        (big, small, x),
    )


def fast_device(
    tokens,
    norm1_gain,
    norm1_shift,
    qkv_weight,
    proj_weight,
    proj_shift,
    norm2_gain,
    norm2_shift,
    router_weight,
    expand_weight,
    expand_shift,
    shrink_weight,
    shrink_shift,
    route_expert,
    route_slot,
    cotangent,
):
    experts = lax.axis_size("expert")
    tensor_count = lax.axis_size("tensor")
    tensor_index = lax.axis_index("tensor")
    tok_count = tokens.shape[0]
    images = tok_count // SEQ
    capacity = tensor_count * (5 * tok_count // (2 * experts * tensor_count) + 1)
    quarter = -(-capacity // (16 * tensor_count)) * 16
    padded = quarter * tensor_count
    width = tokens.shape[1]
    half = width // 2
    token_f = tokens.astype(F32)
    normed, scaled1, inverse1 = normalize(token_f, norm1_gain, norm1_shift)
    normed_b = normed.astype(BF16)
    queries, keys_b, values_b, log_total, context_b = attend_front(normed_b, qkv_weight, images)
    attn_part = jnp.dot(context_b, proj_weight, preferred_element_type=F32).astype(BF16)
    hidden = token_f + tensor_sum(attn_part, 1).astype(F32) + proj_shift
    normed2, scaled2, inverse2 = normalize(hidden, norm2_gain, norm2_shift)
    mixed_b = normed2.astype(BF16)
    logits = jnp.dot(mixed_b, router_weight, preferred_element_type=F32)
    picks = [
        lax.broadcasted_iota(jnp.int32, (tok_count, experts), 1) == route_expert[:, j : j + 1]
        for j in range(2)
    ]
    chosen = [jnp.sum(jnp.where(pick, logits, 0.0), axis=1, keepdims=True) for pick in picks]
    gate_top = jnp.maximum(chosen[0], chosen[1])
    lifted = [jnp.exp(value - gate_top) for value in chosen]
    gates = [value / (lifted[0] + lifted[1]) for value in lifted]
    spots = jnp.where(route_slot >= 0, route_expert * padded + route_slot, -1)
    spots_t = spots.T
    row_ids = lax.broadcasted_iota(jnp.int32, (experts, quarter, 1), 0) * padded
    row_ids = row_ids + lax.broadcasted_iota(jnp.int32, (experts, quarter, 1), 1)
    row_ids = (row_ids + tensor_index * quarter).reshape(experts * quarter, 1)
    hits = [row_ids == spots_t[j][None, :] for j in range(2)]
    chooser = (hits[0] | hits[1]).astype(BF16)
    slot_gate = jnp.sum(
        jnp.where(hits[0], gates[0].reshape(1, -1), 0.0)
        + jnp.where(hits[1], gates[1].reshape(1, -1), 0.0),
        axis=1,
        keepdims=True,
    )
    rows_out = jnp.dot(chooser, mixed_b, preferred_element_type=F32).astype(BF16)
    grad_out = (slot_gate * jnp.dot(chooser, cotangent, preferred_element_type=F32)).astype(BF16)
    received, grad_recv, activ_b, pre_gradb, eshift_g, returned, back_rows = run_experts(
        rows_out.reshape(experts, quarter, width),
        grad_out.reshape(experts, quarter, width),
        expand_weight[0],
        expand_shift,
        shrink_weight[0],
        shrink_shift,
        2,
    )
    received = received.reshape(experts * padded, width)
    grad_recv = grad_recv.reshape(experts * padded, width)
    activ_b = activ_b.reshape(experts * padded, -1)
    pre_gradb = pre_gradb.reshape(experts * padded, -1)
    returned = returned.reshape(experts * padded, half)
    back_rows = back_rows.reshape(experts * padded, half)
    shrink_g = inner_rows(activ_b, grad_recv)
    sshift_g = jnp.sum(grad_recv.astype(F32), axis=0)
    expand_g = inner_rows(received, pre_gradb)
    upstream = cotangent.astype(F32)
    slots = lax.broadcasted_iota(jnp.int32, (tok_count, experts * padded), 1)
    marks = [slots == spots[:, j : j + 1] for j in range(2)]
    mixer = (jnp.where(marks[0], gates[0], 0.0) + jnp.where(marks[1], gates[1], 0.0)).astype(BF16)
    gather = (marks[0] | marks[1]).astype(BF16)
    added = jnp.dot(mixer, returned, preferred_element_type=F32).astype(BF16)
    back = jnp.dot(gather, back_rows, preferred_element_type=F32).astype(BF16)
    cot_half = lax.dynamic_slice(cotangent, (0, (tensor_index // 2) * half), (tok_count, half))
    dots = outer_cols(cot_half, returned)
    gate_part = jnp.stack([jnp.sum(jnp.where(mark, dots, 0.0), axis=1) for mark in marks])
    gate_part = jnp.pad(gate_part, ((0, 6), (0, -tok_count % 128)))
    added, back, gate_full = swap(added, back, gate_part, 4)
    output = hidden + added.astype(F32)
    gate_grad = [gate_full[j, :tok_count].reshape(tok_count, 1) for j in range(2)]
    common = gates[0] * gate_grad[0] + gates[1] * gate_grad[1]
    logit_grad = (
        jnp.where(picks[0], gates[0] * (gate_grad[0] - common), 0.0)
        + jnp.where(picks[1], gates[1] * (gate_grad[1] - common), 0.0)
    ).astype(BF16)
    router_g = inner_rows(logit_grad, mixed_b)
    mixed_grad = back.astype(F32) + outer_cols(logit_grad, router_weight)
    gain2_g = jnp.sum(mixed_grad * scaled2, axis=0)
    shift2_g = jnp.sum(mixed_grad, axis=0)
    hidden_grad = upstream + norm_back(mixed_grad, scaled2, inverse2, norm2_gain)
    pshift_g = jnp.sum(hidden_grad, axis=0)
    hidden_gradb = hidden_grad.astype(BF16)
    context_grad = outer_cols(hidden_gradb, proj_weight).astype(BF16)
    qkv_gradb = attend_back(queries, keys_b, values_b, log_total, context_b, context_grad, images)
    normed_part = outer_cols(qkv_gradb, qkv_weight)
    gain1_g = jnp.sum(normed_part * scaled1, axis=0)
    shift1_g = jnp.sum(normed_part, axis=0)
    qkv_g = inner_rows(normed_b, qkv_gradb)
    proj_g = inner_rows(hidden_gradb, context_b)
    big = jnp.concatenate([qkv_g.astype(BF16), proj_g.astype(BF16)], axis=1)
    wide = big.shape[1]
    small = jnp.concatenate(
        [
            jnp.stack([gain1_g, shift1_g]),
            jnp.stack([pshift_g, gain2_g, shift2_g]) / tensor_count,
            router_g / tensor_count,
        ],
        axis=0,
    )
    names = small.shape[0]
    piece = width // experts
    small = jnp.pad(small, ((0, -names % 8), (0, 0)))
    small = small.reshape(small.shape[0], experts, piece).transpose(1, 0, 2)
    small = jnp.pad(small, ((0, 0), (0, 0), (0, -piece % 128)))
    big, small, normed_sum = final_sums(
        big.reshape(experts, piece, wide), small, normed_part.astype(BF16), 6
    )
    normed_grad = normed_sum.astype(F32)
    tokens_grad = hidden_grad + norm_back(normed_grad, scaled1, inverse1, norm1_gain)
    big = big.reshape(width, wide)
    small = small[:, :, :piece].transpose(1, 0, 2).reshape(-1, width)
    return (
        output,
        tokens_grad,
        small[0],
        small[1],
        big[:, : qkv_g.shape[1]].astype(F32),
        big[:, qkv_g.shape[1] :].T.astype(F32),
        small[2],
        small[3],
        small[4],
        small[5:names].T,
        expand_g[None],
        eshift_g,
        shrink_g[None],
        sshift_g[None],
    )


def solution(mesh):
    small_mesh = mesh.shape["expert"] == 8 and mesh.shape["tensor"] == 4
    on_device = fast_device if small_mesh else plain_device
    return jax.shard_map(
        on_device,
        mesh=mesh,
        in_specs=(
            P("expert", None),
            P(),
            P(),
            P(None, "tensor"),
            P("tensor", None),
            P(),
            P(),
            P(),
            P(),
            P("expert", None, "tensor"),
            P("expert", "tensor"),
            P("expert", "tensor", None),
            P("expert", None),
            P("expert", None),
            P("expert", None),
            P("expert", None),
        ),
        out_specs=(
            P("expert", None),
            P("expert", None),
            P(),
            P(),
            P(None, "tensor"),
            P("tensor", None),
            P(),
            P(),
            P(),
            P(),
            P("expert", None, "tensor"),
            P("expert", "tensor"),
            P("expert", "tensor", None),
            P("expert", None),
        ),
        check_vma=False,
    )
```
